512 devices in a mesh: dp: 32 (over y, x, core), seq: 16 (over z).
Axes of the slice: x: 4, y: 4, z: 16, core: 2. Of those that a mesh axis runs over, the one named last changes fastest.
Arguments:
- queries: bfloat16 [32, 2048, 2048], P('dp', 'seq')
- keys: bfloat16 [32, 2048, 2048], P('dp', 'seq')
- events: bfloat16 [32, 2048, 2048], P('dp', 'seq'), may hold values from -6 to 6
- out_grad: bfloat16 [32, 2048, 2048], P('dp', 'seq'), may hold values from -6 to 6
- segment_ids: int32 [32, 2048], P('dp', 'seq'), may hold values from 0 to 63, never falling along the last dimension, each value on 1 to 512 neighbouring positions
- block_list: int32 [32, 16, 4], P('dp'), may hold values from 0 to 15, as said below
- conv_weight: float32 [64, 2048], replicated, may hold values from -0.75 to 0.75
Outputs:
- query_grad: bfloat16 [32, 2048, 2048], P('dp', 'seq')
- key_grad: bfloat16 [32, 2048, 2048], P('dp', 'seq')
- event_grad: bfloat16 [32, 2048, 2048], P('dp', 'seq')
- filter_grad: float32 [64, 2048], replicated
The draws below stay inside these ranges and needn't reach their ends.
Inputs may be any that keep to these rules, and one draw needn't show every extreme that they name: `block_list`: entry 0 for query block b is b itself; every entry for block b lies in 0 .. b; entries may repeat.
All inputs are finite; a program needn't handle non-finite values.
Results may differ from the reference program's by a relative error of at most 0.015.
Values may be sent and summed in bfloat16 or wider, within the bound.
A program may use at most 64 MiB of HBM per device.

```python
import math
import jax
import jax.numpy as jnp
import numpy as np
from jax import lax

D = 2048
HD = 64
TAPS = 64
BLOCK = 128
NSEL = 4
TOKENS = 2048
NBLK = 16
MICRO = 32
N_DP = 32
N_SEQ = 16


def pair_draw(key):
    key_q = jax.random.fold_in(key, 101)
    key_k = jax.random.fold_in(key, 202)
    shape = (MICRO, TOKENS, D)
    key_f = jax.random.normal(key_k, shape, jnp.float32)
    query_f = jax.random.normal(key_q, shape, jnp.float32)
    return (query_f, key_f)


def draw_queries(key, part):
    return pair_draw(key)[0].astype(jnp.bfloat16)


def draw_keys(key, part):
    return pair_draw(key)[1].astype(jnp.bfloat16)


def draw_block_list(key, part):
    own = jnp.arange(NBLK, dtype=jnp.int32)
    upper = jnp.broadcast_to((own + 1)[None, :, None], (MICRO, NBLK, NSEL - 1))
    others = jax.random.randint(jax.random.fold_in(key, 7), (MICRO, NBLK, NSEL - 1), 0, upper, dtype=jnp.int32)
    first = jnp.broadcast_to(own[None, :, None], (MICRO, NBLK, 1))
    return jnp.concatenate([first, others], axis=2)


def block_levels(key, dims, cuts, smallest, high):
    gain = 1.0
    for axis_at, blocks in cuts:
        steps = jax.random.uniform(jax.random.fold_in(jax.random.fold_in(key, 6), axis_at), (blocks,), jnp.float32, smallest / len(cuts), high / len(cuts))
        gain = gain * jnp.repeat(jnp.exp(steps), dims[axis_at] // blocks).reshape((-1,) + (1,) * (len(dims) - 1 - axis_at))
    return gain


def split_up(count, total, reach, lean):
    portions = [(1 << 20) // math.isqrt(grade ** lean) + 1 for grade in range(2, count + 1)]
    rest, counts = total - reach - (count - 1), [1] * (count - 1)
    while rest > 0:
        movable = [i for i in range(count - 1) if counts[i] < reach]
        whole, budget = sum([portions[i] for i in movable]), rest
        for i in movable:
            extra = min(reach - counts[i], max(1, budget * portions[i] // whole), rest)
            counts[i] = counts[i] + extra
            rest = rest - extra
    return np.array([reach] + counts)


def ragged(stream_key, amount, total, reach, slope):
    if amount == 2:
        one = jax.random.randint(stream_key, (), max(1, total - reach), min(reach, total - 1) + 1)
        return jnp.stack([one, total - one])
    tallies = jnp.asarray(split_up(amount, total, reach, slope), jnp.int32)
    couples = (amount - 1) // 2
    source_of, receiver = tallies[1:1 + 2 * couples:2], tallies[2:2 + 2 * couples:2]
    slack = jnp.minimum(source_of - 1, reach - receiver)
    moved = jax.random.randint(jax.random.fold_in(stream_key, 1), (couples,), 0, 1 << 20) % (slack + 1)
    tallies = tallies.at[1:1 + 2 * couples:2].set(source_of - moved).at[2:2 + 2 * couples:2].set(receiver + moved)
    return tallies[jax.random.permutation(jax.random.fold_in(stream_key, 2), amount)]


def bell_draw(rng, shape, scale, most, shards=(), kind=jnp.bfloat16):
    entries = jax.random.normal(rng, shape, jnp.float32) * scale
    if len(shards) > 0:
        entries = block_levels(rng, shape, shards, -0.22, 0.18) * entries
    return jnp.clip(entries, min=-most, max=most).astype(kind)


def setup_inputs(seed: int = 0) -> dict:
    key_of = jax.random.split(jax.random.key(seed), 8)
    return {
        "queries": draw_queries(jax.random.fold_in(key_of[7], 71), 0),
        "keys": draw_keys(jax.random.fold_in(key_of[7], 71), 0),
        "events": bell_draw(key_of[2], (MICRO, TOKENS, D), 1.0, 6.0, ((0, 32), (1, 16))),
        "out_grad": bell_draw(key_of[3], (MICRO, TOKENS, D), 1.0, 6.0, ((0, 32), (1, 16))),
        "segment_ids": jax.vmap(lambda own: jnp.searchsorted(jnp.cumsum(ragged(own, TOKENS // 32, TOKENS, 4 * BLOCK, 2)), jnp.arange(TOKENS), side="right"))(jax.random.split(key_of[4], MICRO)).reshape((MICRO, TOKENS)).astype(jnp.int32),
        "block_list": draw_block_list(jax.random.fold_in(key_of[7], 71), 0),
        "conv_weight": bell_draw(key_of[6], (TAPS, D), TAPS ** -0.5, 0.75, (), jnp.float32),
    }


def contract(form, left, right, exact):
    return jnp.einsum(form, left.astype(jnp.float32), right.astype(jnp.float32), precision=lax.Precision.HIGHEST)


def causal_conv(padded, ids_ext, weight, count):
    taps = weight.shape[0]
    own = lax.dynamic_slice_in_dim(ids_ext, taps - 1, count, 0)

    def add_tap(step, total):
        piece = lax.dynamic_slice_in_dim(padded, taps - 1 - step, count, 0).astype(jnp.float32)
        ids_piece = lax.dynamic_slice_in_dim(ids_ext, taps - 1 - step, count, 0)
        tap_row = lax.dynamic_slice_in_dim(weight, step, 1, 0)
        return total + jnp.where((ids_piece == own)[:, None], piece * tap_row, 0.0)

    return lax.fori_loop(0, taps, add_tap, jnp.zeros((count, padded.shape[1]), jnp.float32))


def anti_conv(padded, ids_ext, weight, count):
    taps = weight.shape[0]
    own = lax.dynamic_slice_in_dim(ids_ext, 0, count, 0)

    def add_tap(step, total):
        piece = lax.dynamic_slice_in_dim(padded, step, count, 0).astype(jnp.float32)
        ids_piece = lax.dynamic_slice_in_dim(ids_ext, step, count, 0)
        tap_row = lax.dynamic_slice_in_dim(weight, step, 1, 0)
        return total + jnp.where((ids_piece == own)[:, None], piece * tap_row, 0.0)

    return lax.fori_loop(0, taps, add_tap, jnp.zeros((count, padded.shape[1]), jnp.float32))


def tap_gradient(grad, padded, ids_ext, taps):
    count = grad.shape[0]
    own = lax.dynamic_slice_in_dim(ids_ext, taps - 1, count, 0)
    grad_wide = grad.astype(jnp.float32)

    def one_tap(step):
        piece = lax.dynamic_slice_in_dim(padded, taps - 1 - step, count, 0).astype(jnp.float32)
        ids_piece = lax.dynamic_slice_in_dim(ids_ext, taps - 1 - step, count, 0)
        return jnp.sum(jnp.where((ids_piece == own)[:, None], piece * grad_wide, 0.0), axis=0)

    return lax.map(one_tap, jnp.arange(taps, dtype=jnp.int32))


def block_attention(query, key_rows, value, grad, ids, blist, block):
    tokens, head_dim = query.shape
    nblk = tokens // block
    nsel = blist.shape[1]
    scale = head_dim ** -0.5
    same = blist[:, :, None] == blist[:, None, :]
    before = jnp.arange(nsel)[None, :, None] > jnp.arange(nsel)[None, None, :]
    fresh = jnp.logical_not(jnp.any(same & before, axis=2))
    chosen = (blist[:, :, None] == jnp.arange(nblk, dtype=jnp.int32)[None, None, :]) & fresh[:, :, None]
    picker = chosen.astype(jnp.bfloat16)
    q_blk = query.reshape(nblk, block, head_dim)
    k_blk = key_rows.reshape(nblk, block, head_dim)
    v_blk = value.reshape(nblk, block, head_dim)
    g_blk = grad.reshape(nblk, block, head_dim)
    k_sel = contract('bjc,cmd->bjmd', picker, k_blk, False).astype(jnp.bfloat16)
    v_sel = contract('bjc,cmd->bjmd', picker, v_blk, False).astype(jnp.bfloat16)
    id_blk = ids.reshape(nblk, block)
    id_sel = jnp.sum(jnp.where(chosen[:, :, :, None], id_blk[None, None, :, :], 0), axis=2)
    q_pos = jnp.arange(nblk, dtype=jnp.int32)[:, None] * block + jnp.arange(block, dtype=jnp.int32)[None, :]
    k_pos = blist[:, :, None] * block + jnp.arange(block, dtype=jnp.int32)[None, None, :]
    allowed = fresh[:, None, :, None] & (k_pos[:, None] <= q_pos[:, :, None, None]) & (id_sel[:, None] == id_blk[:, :, None, None])
    scores = contract('bid,bjmd->bijm', q_blk, k_sel, False) * scale
    scores = jnp.where(allowed, scores, -1e30)
    top = jnp.max(scores, axis=(2, 3), keepdims=True)
    weights = jnp.where(allowed, jnp.exp(scores - top), 0.0)
    probs = weights / jnp.sum(weights, axis=(2, 3), keepdims=True)
    probs_low = probs.astype(jnp.bfloat16)
    attended = contract('bijm,bjmd->bid', probs_low, v_sel, False)
    delta = jnp.sum(g_blk.astype(jnp.float32) * attended, axis=2)
    dprobs = contract('bid,bjmd->bijm', g_blk, v_sel, False)
    dscores = (probs * (dprobs - delta[:, :, None, None])).astype(jnp.bfloat16)
    q_grad = (contract('bijm,bjmd->bid', dscores, k_sel, False) * scale).astype(jnp.bfloat16)
    k_slot = contract('bijm,bid->bjmd', dscores, q_blk, False) * scale
    v_slot = contract('bijm,bid->bjmd', probs_low, g_blk, False)
    spread = chosen.astype(jnp.float32)
    k_grad = contract('bjc,bjmd->cmd', spread, k_slot, True).astype(jnp.bfloat16)
    v_grad = contract('bjc,bjmd->cmd', spread, v_slot, True).astype(jnp.bfloat16)
    return (q_grad.reshape(tokens, head_dim), k_grad.reshape(tokens, head_dim), v_grad.reshape(tokens, head_dim))


def heads_attention(query, key_rows, value, grad, ids, blist, head_dim, block):
    tokens, width = query.shape
    heads = width // head_dim

    def split(array):
        return array.reshape(tokens, heads, head_dim).transpose(1, 0, 2)

    def join(array):
        return array.transpose(1, 0, 2).reshape(tokens, width)

    def one_head(item):
        return block_attention(item[0], item[1], item[2], item[3], ids, blist, block)

    q_grad, k_grad, v_grad = lax.map(one_head, (split(query), split(key_rows), split(value), split(grad)))
    return join(q_grad), join(k_grad), join(v_grad)


def reference(queries, keys, events, out_grad, segment_ids, block_list, conv_weight):
    taps = conv_weight.shape[0]

    def one_batch(item):
        query, key_rows, feats, grad, ids, blist = item
        rim = jnp.zeros((taps - 1,), jnp.int32)
        ids_all = jnp.concatenate([rim, ids + 1, rim])
        left_ids = ids_all[:TOKENS + taps - 1]
        right_ids = ids_all[taps - 1:]
        padded = jnp.concatenate([jnp.zeros((taps - 1, D), jnp.bfloat16), feats], axis=0)
        values = causal_conv(padded, left_ids, conv_weight, TOKENS).astype(jnp.bfloat16)
        q_grad, k_grad, v_grad = heads_attention(query, key_rows, values, grad, ids, blist, HD, BLOCK)
        after = jnp.concatenate([v_grad, jnp.zeros((taps - 1, D), jnp.bfloat16)], axis=0)
        e_grad = anti_conv(after, right_ids, conv_weight, TOKENS).astype(jnp.bfloat16)
        f_grad = tap_gradient(v_grad, padded, left_ids, taps)
        return q_grad, k_grad, e_grad, f_grad

    q_all, k_all, e_all, f_all = lax.map(one_batch, (queries, keys, events, out_grad, segment_ids, block_list))
    return q_all, k_all, e_all, jnp.sum(f_all, axis=0) / (N_DP * N_SEQ)
```

```python
import jax
import jax.numpy as jnp
from jax import lax
from jax.experimental import pallas as pl
from jax.experimental.pallas import tpu as pltpu
from jax.sharding import PartitionSpec as P

MESH = pl.DeviceIdType.MESH

HD = 64
BLOCK = 128


def shifted(value, axis, steps):
    count = lax.axis_size(axis)
    initial, last = (max(0, -steps), min(count, count - steps))
    return lax.ppermute(value, axis, [(source, source + steps) for source in range(initial, last)])


def contract(form, left, right, exact):
    if exact:
        return jnp.einsum(
            form, left, right, precision=lax.Precision.HIGHEST, preferred_element_type=jnp.float32
        )
    return jnp.einsum(form, left, right, preferred_element_type=jnp.float32)


def causal_conv(padded, ids_ext, weight, count):
    taps = weight.shape[0]
    own = ids_ext[taps - 1 : taps - 1 + count]
    total = jnp.zeros((count, padded.shape[1]), jnp.float32)
    for step in range(taps):
        begin = taps - 1 - step
        piece = padded[begin : begin + count].astype(jnp.float32)
        match = (ids_ext[begin : begin + count] == own)[:, None]
        total = total + jnp.where(match, piece * weight[step : step + 1], 0.0)
    return total


def anti_conv(padded, ids_ext, weight, count):
    taps = weight.shape[0]
    own = ids_ext[0:count]
    total = jnp.zeros((count, padded.shape[1]), jnp.float32)
    for step in range(taps):
        piece = padded[step : step + count].astype(jnp.float32)
        match = (ids_ext[step : step + count] == own)[:, None]
        total = total + jnp.where(match, piece * weight[step : step + 1], 0.0)
    return total


def tap_gradient(grad, padded, ids_ext, taps):
    count = grad.shape[0]
    own = ids_ext[taps - 1 : taps - 1 + count]
    grad_wide = grad.astype(jnp.float32)
    sums = []
    for step in range(taps):
        begin = taps - 1 - step
        piece = padded[begin : begin + count].astype(jnp.float32)
        match = (ids_ext[begin : begin + count] == own)[:, None]
        sums.append(jnp.sum(jnp.where(match, piece * grad_wide, 0.0), axis=0))
    return jnp.stack(sums, axis=0)


def block_attention(query, key_rows, value, grad, ids, blist, block):
    tokens, head_dim = query.shape
    nblk = tokens // block
    nsel = blist.shape[1]
    scale = head_dim ** (-0.5)
    same = blist[:, :, None] == blist[:, None, :]
    before = jnp.arange(nsel)[None, :, None] > jnp.arange(nsel)[None, None, :]
    fresh = jnp.logical_not(jnp.any(same & before, axis=2))
    chosen = (blist[:, :, None] == jnp.arange(nblk, dtype=jnp.int32)[None, None, :]) & fresh[
        :, :, None
    ]
    picker = chosen.astype(jnp.bfloat16)
    q_blk = query.reshape(nblk, block, head_dim)
    k_blk = key_rows.reshape(nblk, block, head_dim)
    v_blk = value.reshape(nblk, block, head_dim)
    g_blk = grad.reshape(nblk, block, head_dim)
    k_sel = contract("bjc,cmd->bjmd", picker, k_blk, False).astype(jnp.bfloat16)
    v_sel = contract("bjc,cmd->bjmd", picker, v_blk, False).astype(jnp.bfloat16)
    id_blk = ids.reshape(nblk, block)
    id_sel = jnp.sum(jnp.where(chosen[:, :, :, None], id_blk[None, None, :, :], 0), axis=2)
    q_pos = (
        jnp.arange(nblk, dtype=jnp.int32)[:, None] * block
        + jnp.arange(block, dtype=jnp.int32)[None, :]
    )
    k_pos = blist[:, :, None] * block + jnp.arange(block, dtype=jnp.int32)[None, None, :]
    allowed = (
        fresh[:, None, :, None]
        & (k_pos[:, None] <= q_pos[:, :, None, None])
        & (id_sel[:, None] == id_blk[:, :, None, None])
    )
    scores = contract("bid,bjmd->bijm", q_blk, k_sel, False) * scale
    scores = jnp.where(allowed, scores, -1e30)
    top = jnp.max(scores, axis=(2, 3), keepdims=True)
    weights = jnp.where(allowed, jnp.exp(scores - top), 0.0)
    probs = weights / jnp.sum(weights, axis=(2, 3), keepdims=True)
    probs_low = probs.astype(jnp.bfloat16)
    attended = contract("bijm,bjmd->bid", probs_low, v_sel, False)
    delta = jnp.sum(g_blk.astype(jnp.float32) * attended, axis=2)
    dprobs = contract("bid,bjmd->bijm", g_blk, v_sel, False)
    dscores = (probs * (dprobs - delta[:, :, None, None])).astype(jnp.bfloat16)
    q_grad = (contract("bijm,bjmd->bid", dscores, k_sel, False) * scale).astype(jnp.bfloat16)
    k_slot = contract("bijm,bid->bjmd", dscores, q_blk, False) * scale
    v_slot = contract("bijm,bid->bjmd", probs_low, g_blk, False)
    spread = chosen.astype(jnp.float32)
    k_grad = contract("bjc,bjmd->cmd", spread, k_slot, True).astype(jnp.bfloat16)
    v_grad = contract("bjc,bjmd->cmd", spread, v_slot, True).astype(jnp.bfloat16)
    return (
        q_grad.reshape(tokens, head_dim),
        k_grad.reshape(tokens, head_dim),
        v_grad.reshape(tokens, head_dim),
    )


def heads_attention(query, key_rows, value, grad, ids, blist, head_dim, block):
    tokens, width = query.shape
    heads = width // head_dim

    def split(array):
        return array.reshape(tokens, heads, head_dim).transpose(1, 0, 2)

    def join(array):
        return array.transpose(1, 0, 2).reshape(tokens, width)

    def one_head(item):
        return block_attention(item[0], item[1], item[2], item[3], ids, blist, block)

    q_grad, k_grad, v_grad = lax.map(
        one_head, (split(query), split(key_rows), split(value), split(grad))
    )
    return (join(q_grad), join(k_grad), join(v_grad))


def spread_sum(local, scale):
    n_dp, n_seq = lax.axis_size("dp"), lax.axis_size("seq")
    taps, width = local.shape
    lanes = 128
    parts = width // lanes
    split = n_dp // parts
    rows = taps // split

    def kernel(x_ref, o_ref, mine, got, part, gotz, tot, done, s1, r1, s2, r2, s3, r3):
        me = lax.axis_index("dp")
        z = lax.axis_index("seq")
        barrier = pltpu.get_barrier_semaphore()

        def greet_dp(i, _):
            pl.semaphore_signal(barrier, inc=1, device_id={"dp": lax.rem(me + i, n_dp)}, device_id_type=MESH)
            return 0

        def greet_z(i, _):
            pl.semaphore_signal(barrier, inc=1, device_id={"seq": lax.rem(z + i, n_seq)}, device_id_type=MESH)
            return 0

        lax.fori_loop(1, n_dp, greet_dp, 0)
        lax.fori_loop(1, n_seq, greet_z, 0)
        for j in range(n_dp):
            col, row = (j // split) * lanes, (j % split) * rows
            mine[j] = x_ref[row : row + rows, col : col + lanes].astype(jnp.bfloat16)
        pl.semaphore_wait(barrier, n_dp + n_seq - 2)

        def out1(i):
            to = lax.rem(me + i, n_dp)
            return pltpu.make_async_remote_copy(
                src_ref=mine.at[to], dst_ref=got.at[me], send_sem=s1.at[i], recv_sem=r1.at[me],
                device_id={"dp": to}, device_id_type=MESH)

        def in1(i):
            src = lax.rem(me + i, n_dp)
            return pltpu.make_async_remote_copy(
                src_ref=mine.at[src], dst_ref=got.at[src], send_sem=s1.at[i], recv_sem=r1.at[src],
                device_id={"dp": src}, device_id_type=MESH)

        def out2(i):
            to = lax.rem(z + i, n_seq)
            return pltpu.make_async_remote_copy(
                src_ref=part, dst_ref=gotz.at[z], send_sem=s2.at[i], recv_sem=r2.at[z],
                device_id={"seq": to}, device_id_type=MESH)

        def in2(i):
            src = lax.rem(z + i, n_seq)
            return pltpu.make_async_remote_copy(
                src_ref=part, dst_ref=gotz.at[src], send_sem=s2.at[i], recv_sem=r2.at[src],
                device_id={"seq": src}, device_id_type=MESH)

        def out3(i):
            to = lax.rem(me + i, n_dp)
            return pltpu.make_async_remote_copy(
                src_ref=tot, dst_ref=done.at[me], send_sem=s3.at[i], recv_sem=r3.at[me],
                device_id={"dp": to}, device_id_type=MESH)

        def in3(i):
            src = lax.rem(me + i, n_dp)
            return pltpu.make_async_remote_copy(
                src_ref=tot, dst_ref=done.at[src], send_sem=s3.at[i], recv_sem=r3.at[src],
                device_id={"dp": src}, device_id_type=MESH)

        def start(make, count):
            def body(i, _):
                make(i).start()
                return 0
            lax.fori_loop(1, count, body, 0)

        def sent(make, count):
            def body(i, _):
                make(i).wait_send()
                return 0
            lax.fori_loop(1, count, body, 0)

        def landed(make, count):
            def body(i, _):
                make(i).wait_recv()
                return 0
            lax.fori_loop(1, count, body, 0)

        start(out1, n_dp)
        got[me] = mine[me]
        landed(in1, n_dp)
        total = got[0].astype(jnp.float32)
        for j in range(1, n_dp):
            total = total + got[j].astype(jnp.float32)
        part[...] = total.astype(jnp.bfloat16)
        start(out2, n_seq)
        gotz[z] = part[...]
        landed(in2, n_seq)
        total = gotz[0].astype(jnp.float32)
        for j in range(1, n_seq):
            total = total + gotz[j].astype(jnp.float32)
        tot[...] = (total * scale).astype(jnp.bfloat16)
        start(out3, n_dp)
        done[me] = tot[...]
        landed(in3, n_dp)
        for j in range(n_dp):
            col, row = (j // split) * lanes, (j % split) * rows
            o_ref[row : row + rows, col : col + lanes] = done[j].astype(jnp.float32)
        sent(out1, n_dp)
        sent(out2, n_seq)
        sent(out3, n_dp)

    piece = (rows, lanes)
    return pl.pallas_call(
        kernel,
        out_shape=jax.ShapeDtypeStruct((taps, width), jnp.float32),
        in_specs=[pl.BlockSpec(memory_space=pltpu.VMEM)],
        out_specs=pl.BlockSpec(memory_space=pltpu.VMEM),
        scratch_shapes=[
            pltpu.VMEM((n_dp,) + piece, jnp.bfloat16),
            pltpu.VMEM((n_dp,) + piece, jnp.bfloat16),
            pltpu.VMEM(piece, jnp.bfloat16),
            pltpu.VMEM((n_seq,) + piece, jnp.bfloat16),
            pltpu.VMEM(piece, jnp.bfloat16),
            pltpu.VMEM((n_dp,) + piece, jnp.bfloat16),
            pltpu.SemaphoreType.DMA((n_dp,)),
            pltpu.SemaphoreType.DMA((n_dp,)),
            pltpu.SemaphoreType.DMA((n_seq,)),
            pltpu.SemaphoreType.DMA((n_seq,)),
            pltpu.SemaphoreType.DMA((n_dp,)),
            pltpu.SemaphoreType.DMA((n_dp,)),
        ],
        compiler_params=pltpu.CompilerParams(collective_id=1, has_side_effects=True),
        name="spread_sum",
    )(local)


def per_device(queries, keys, events, out_grad, segment_ids, block_list, conv_weight):
    query = queries[0]
    key_rows = keys[0]
    feats = events[0]
    grad = out_grad[0]
    blist = block_list[0]
    rows, width = query.shape
    taps = conv_weight.shape[0]
    shards = lax.axis_size("dp") * lax.axis_size("seq")
    position = lax.axis_index("seq")
    all_ids = lax.all_gather(segment_ids, "seq", axis=1, tiled=True)[0]
    rim = jnp.zeros((taps - 1,), jnp.int32)
    ids_all = jnp.concatenate([rim, all_ids + 1, rim])
    left_ids = lax.dynamic_slice_in_dim(ids_all, position * rows, rows + taps - 1, 0)
    right_ids = lax.dynamic_slice_in_dim(ids_all, position * rows + taps - 1, rows + taps - 1, 0)
    earlier = shifted(feats[rows - (taps - 1) :], "seq", 1)
    padded = jnp.concatenate([earlier, feats], axis=0)
    values = causal_conv(padded, left_ids, conv_weight, rows).astype(jnp.bfloat16)
    head_q, head_k, head_v, head_g = (
        lax.all_to_all(query, "seq", split_axis=1, concat_axis=0, tiled=True),
        lax.all_to_all(key_rows, "seq", split_axis=1, concat_axis=0, tiled=True),
        lax.all_to_all(values, "seq", split_axis=1, concat_axis=0, tiled=True),
        lax.all_to_all(grad, "seq", split_axis=1, concat_axis=0, tiled=True),
    )
    q_grad, k_grad, v_grad = heads_attention(
        head_q, head_k, head_v, head_g, all_ids, blist, HD, BLOCK
    )
    q_back, k_back, v_back = (
        lax.all_to_all(q_grad, "seq", split_axis=0, concat_axis=1, tiled=True),
        lax.all_to_all(k_grad, "seq", split_axis=0, concat_axis=1, tiled=True),
        lax.all_to_all(v_grad, "seq", split_axis=0, concat_axis=1, tiled=True),
    )
    later = shifted(v_back[: taps - 1], "seq", -1)
    after = jnp.concatenate([v_back, later], axis=0)
    e_grad = anti_conv(after, right_ids, conv_weight, rows).astype(jnp.bfloat16)
    f_local = tap_gradient(v_back, padded, left_ids, taps)
    f_grad = spread_sum(f_local, 1.0 / shards)
    return (q_back[None], k_back[None], e_grad[None], f_grad)


def solution(mesh):
    in_specs = (
        P("dp", "seq", None),
        P("dp", "seq", None),
        P("dp", "seq", None),
        P("dp", "seq", None),
        P("dp", "seq"),
        P("dp", None, None),
        P(),
    )
    out_specs = (P("dp", "seq", None), P("dp", "seq", None), P("dp", "seq", None), P())
    return jax.shard_map(
        per_device, mesh=mesh, in_specs=in_specs, out_specs=out_specs, check_vma=False
    )
```

```python
import jax
import jax.numpy as jnp
from jax import lax
from jax.experimental import pallas as pl
from jax.experimental.pallas import tpu as pltpu
from jax.sharding import PartitionSpec as P

HD = 64
REACH = 4
LANES = 128
RIM = 64
GROUP = 2
MESH = pl.DeviceIdType.MESH


def spread_sum(local, scale):
    n_dp, n_seq = lax.axis_size("dp"), lax.axis_size("seq")
    taps, width = local.shape
    lanes = 128
    parts = width // lanes
    split = n_dp // parts
    rows = taps // split

    def kernel(x_ref, o_ref, mine, got, part, gotz, tot, done, s1, r1, s2, r2, s3, r3):
        me = lax.axis_index("dp")
        z = lax.axis_index("seq")
        barrier = pltpu.get_barrier_semaphore()

        def greet_dp(i, _):
            pl.semaphore_signal(barrier, inc=1, device_id={"dp": lax.rem(me + i, n_dp)}, device_id_type=MESH)
            return 0

        def greet_z(i, _):
            pl.semaphore_signal(barrier, inc=1, device_id={"seq": lax.rem(z + i, n_seq)}, device_id_type=MESH)
            return 0

        lax.fori_loop(1, n_dp, greet_dp, 0)
        lax.fori_loop(1, n_seq, greet_z, 0)
        for j in range(n_dp):
            col, row = (j // split) * lanes, (j % split) * rows
            mine[j] = x_ref[row : row + rows, col : col + lanes].astype(jnp.bfloat16)
        pl.semaphore_wait(barrier, n_dp + n_seq - 2)

        def out1(i):
            to = lax.rem(me + i, n_dp)
            return pltpu.make_async_remote_copy(
                src_ref=mine.at[to], dst_ref=got.at[me], send_sem=s1.at[i], recv_sem=r1.at[me],
                device_id={"dp": to}, device_id_type=MESH)

        def in1(i):
            src = lax.rem(me + i, n_dp)
            return pltpu.make_async_remote_copy(
                src_ref=mine.at[src], dst_ref=got.at[src], send_sem=s1.at[i], recv_sem=r1.at[src],
                device_id={"dp": src}, device_id_type=MESH)

        def out2(i):
            to = lax.rem(z + i, n_seq)
            return pltpu.make_async_remote_copy(
                src_ref=part, dst_ref=gotz.at[z], send_sem=s2.at[i], recv_sem=r2.at[z],
                device_id={"seq": to}, device_id_type=MESH)

        def in2(i):
            src = lax.rem(z + i, n_seq)
            return pltpu.make_async_remote_copy(
                src_ref=part, dst_ref=gotz.at[src], send_sem=s2.at[i], recv_sem=r2.at[src],
                device_id={"seq": src}, device_id_type=MESH)

        def out3(i):
            to = lax.rem(me + i, n_dp)
            return pltpu.make_async_remote_copy(
                src_ref=tot, dst_ref=done.at[me], send_sem=s3.at[i], recv_sem=r3.at[me],
                device_id={"dp": to}, device_id_type=MESH)

        def in3(i):
            src = lax.rem(me + i, n_dp)
            return pltpu.make_async_remote_copy(
                src_ref=tot, dst_ref=done.at[src], send_sem=s3.at[i], recv_sem=r3.at[src],
                device_id={"dp": src}, device_id_type=MESH)

        def start(make, count):
            def body(i, _):
                make(i).start()
                return 0
            lax.fori_loop(1, count, body, 0)

        def sent(make, count):
            def body(i, _):
                make(i).wait_send()
                return 0
            lax.fori_loop(1, count, body, 0)

        def landed(make, count):
            def body(i, _):
                make(i).wait_recv()
                return 0
            lax.fori_loop(1, count, body, 0)

        start(out1, n_dp)
        got[me] = mine[me]
        landed(in1, n_dp)
        total = got[0].astype(jnp.float32)
        for j in range(1, n_dp):
            total = total + got[j].astype(jnp.float32)
        part[...] = total.astype(jnp.bfloat16)
        start(out2, n_seq)
        gotz[z] = part[...]
        landed(in2, n_seq)
        total = gotz[0].astype(jnp.float32)
        for j in range(1, n_seq):
            total = total + gotz[j].astype(jnp.float32)
        tot[...] = (total * scale).astype(jnp.bfloat16)
        start(out3, n_dp)
        done[me] = tot[...]
        landed(in3, n_dp)
        for j in range(n_dp):
            col, row = (j // split) * lanes, (j % split) * rows
            o_ref[row : row + rows, col : col + lanes] = done[j].astype(jnp.float32)
        sent(out1, n_dp)
        sent(out2, n_seq)
        sent(out3, n_dp)

    piece = (rows, lanes)
    return pl.pallas_call(
        kernel,
        out_shape=jax.ShapeDtypeStruct((taps, width), jnp.float32),
        in_specs=[pl.BlockSpec(memory_space=pltpu.VMEM)],
        out_specs=pl.BlockSpec(memory_space=pltpu.VMEM),
        scratch_shapes=[
            pltpu.VMEM((n_dp,) + piece, jnp.bfloat16),
            pltpu.VMEM((n_dp,) + piece, jnp.bfloat16),
            pltpu.VMEM(piece, jnp.bfloat16),
            pltpu.VMEM((n_seq,) + piece, jnp.bfloat16),
            pltpu.VMEM(piece, jnp.bfloat16),
            pltpu.VMEM((n_dp,) + piece, jnp.bfloat16),
            pltpu.SemaphoreType.DMA((n_dp,)),
            pltpu.SemaphoreType.DMA((n_dp,)),
            pltpu.SemaphoreType.DMA((n_seq,)),
            pltpu.SemaphoreType.DMA((n_seq,)),
            pltpu.SemaphoreType.DMA((n_dp,)),
            pltpu.SemaphoreType.DMA((n_dp,)),
        ],
        compiler_params=pltpu.CompilerParams(collective_id=1, has_side_effects=True),
        name="spread_sum",
    )(local)


def timeline(query, key_rows, feats, grad, ids, picked, weight):
    n_seq = lax.axis_size("seq")
    rows, width = query.shape
    taps = weight.shape[0]
    tiles = width // LANES
    chunks = tiles // GROUP
    scale = HD ** (-0.5)
    span = (REACH + 1) * rows
    shifted_rows = rows + RIM - 8
    f32, bf16 = jnp.float32, jnp.bfloat16

    def kernel(
        q_ref, k_ref, e_ref, g_ref, id_ref, pick_ref, w_ref,
        dq_ref, dk_ref, de_ref, f_ref,
        win, part, out_buf, in_buf, e_halo, v_halo, vg, e_src,
        id_src, id_buf, cap, left, right, ext, moved,
        win_s, win_r, back_s, back_r, eh_s, eh_r, vh_s, vh_r, id_s, id_r,
    ):
        me = lax.axis_index("seq")

        def at(offset):
            return lax.rem(me + offset + n_seq, n_seq)

        up, down = at(1), at(-1)

        def remote(src, dst, send, recv, to):
            return pltpu.make_async_remote_copy(
                src_ref=src, dst_ref=dst, send_sem=send, recv_sem=recv,
                device_id={"seq": to}, device_id_type=MESH,
            )

        def cols(tile):
            return pl.ds(pl.multiple_of(tile * LANES, LANES), LANES)

        def group(c):
            return pl.ds(c * GROUP, GROUP)

        def fwd(c, d):
            return remote(
                win.at[:, group(c), pl.ds((d - 1) * rows, rows), :],
                win.at[:, group(c), pl.ds(d * rows, rows), :],
                win_s.at[c, d - 1], win_r.at[c, d - 1], up,
            )

        def back(c, d):
            return remote(
                out_buf.at[:, group(c), pl.ds((d - 1) * rows, rows), :],
                in_buf.at[:, group(c), pl.ds((d - 1) * rows, rows), :],
                back_s.at[c, d - 1], back_r.at[c, d - 1], down,
            )

        def events_halo(c):
            return remote(
                e_src.at[group(c)], e_halo.at[group(c)], eh_s.at[c], eh_r.at[c], up
            )

        def grads_halo(c):
            return remote(
                vg.at[group(c), pl.ds(0, RIM), :], v_halo.at[group(c)], vh_s.at[c], vh_r.at[c], down
            )

        def ids_to(slot):
            to = down if slot == 0 else at(slot)
            return remote(id_src, id_buf.at[slot], id_s.at[slot], id_r.at[slot], to)

        barrier = pltpu.get_barrier_semaphore()
        for offset in range(1, REACH + 1):
            for to in (at(offset), at(-offset)):
                pl.semaphore_signal(barrier, inc=1, device_id={"seq": to}, device_id_type=MESH)
        own_ids = id_ref[...].astype(f32)
        id_src[...] = jnp.broadcast_to(own_ids, id_src.shape)

        def stage(tile, _):
            win[0, tile, pl.ds(0, rows), :] = k_ref[:, cols(tile)]
            e_src[tile] = e_ref[pl.ds(rows - RIM, RIM), cols(tile)]
            return 0

        lax.fori_loop(0, tiles, stage, 0)
        pl.semaphore_wait(barrier, 2 * REACH)
        for slot in range(REACH + 1):
            ids_to(slot).start()

        def start_halo(c, _):
            events_halo(c).start()
            return 0

        lax.fori_loop(0, chunks, start_halo, 0)
        for slot in range(REACH + 1):
            ids_to(slot).wait_recv()

        square = (rows, rows)
        own_row = jnp.broadcast_to(own_ids, square)

        def same(row):
            col = jnp.broadcast_to(row, square).T
            return jnp.where(col == own_row, 1.0, 0.0)

        s_at = lax.broadcasted_iota(jnp.int32, square, 0)
        r_at = lax.broadcasted_iota(jnp.int32, square, 1)
        here = same(own_ids)
        low = jnp.where(s_at <= r_at, here, 0.0)
        high = jnp.where(s_at >= r_at, here, 0.0)
        before = same(id_buf[1][0:1]) * jnp.where(me > 0, 1.0, 0.0)
        after = same(id_buf[0][0:1]) * jnp.where(me < n_seq - 1, 1.0, 0.0)
        reach_left = jnp.sum(low, axis=0, keepdims=True) + jnp.sum(before, axis=0, keepdims=True) - 1.0
        reach_right = jnp.sum(high, axis=0, keepdims=True) + jnp.sum(after, axis=0, keepdims=True) - 1.0
        left[...] = jnp.broadcast_to(reach_left, square).T
        right[...] = jnp.broadcast_to(reach_right, square).T
        for d in range(REACH + 1):
            open_pairs = low if d == 0 else same(id_buf[d][0:1])
            open_pairs = open_pairs * jnp.broadcast_to(pick_ref[d : d + 1, :], square)
            limit = jnp.where(open_pairs > 0.5, 3.0e38, -1.0e30)
            cap[d * rows : (d + 1) * rows, 0:rows] = limit
            cap[d * rows : (d + 1) * rows, rows : 2 * rows] = limit

        def shift_back():
            for k in range(8):
                moved[k] = ext[8 - k : 8 - k + shifted_rows, :]

        def load_events(tile):
            ext[0:RIM, :] = e_halo[tile].astype(f32)
            ext[RIM : RIM + rows, :] = e_ref[:, cols(tile)].astype(f32)
            shift_back()

        def taps_at(q, tile):
            return w_ref[pl.ds(pl.multiple_of(q * 8, 8), 8), cols(tile)]

        def conv(tile):
            load_events(tile)
            reach = left[...]

            def body(q, total):
                tap_rows = taps_at(q, tile)
                base = pl.multiple_of(RIM - 8 - 8 * q, 8)
                first = (q * 8).astype(f32)
                for k in range(8):
                    piece = moved[k, pl.ds(base, rows), :]
                    total = total + jnp.where(reach >= first + k, piece * tap_rows[k : k + 1, :], 0.0)
                return total

            total = lax.fori_loop(0, taps // 8, body, jnp.zeros((rows, LANES), f32))
            win[1, tile, pl.ds(0, rows), :] = total.astype(bf16)

        def conv_chunk(c):
            events_halo(c).wait_recv()
            for j in range(GROUP):
                conv(c * GROUP + j)

        def attend(tile):
            lane = lax.broadcasted_iota(jnp.int32, (rows, LANES), 1)
            first = lane < HD

            def pair(ref):
                both = ref[:, cols(tile)].astype(f32)
                return jnp.concatenate(
                    [jnp.where(first, both, 0.0), jnp.where(first, 0.0, both)], axis=0
                ).astype(bf16)

            q2, g2 = pair(q_ref), pair(g_ref)
            keys, vals = win[0, tile], win[1, tile]
            last = (((1,), (1,)), ((), ()))
            scores = lax.dot_general(keys, q2, last, preferred_element_type=f32)
            scores = jnp.minimum(scores * scale, cap[...])
            top = jnp.max(scores, axis=0, keepdims=True)
            raw = jnp.exp(scores - top)
            probs = raw * (1.0 / jnp.sum(raw, axis=0, keepdims=True))
            low_probs = probs.astype(bf16)
            dprobs = lax.dot_general(vals, g2, last, preferred_element_type=f32)
            delta = jnp.sum(low_probs.astype(f32) * dprobs, axis=0, keepdims=True)
            dscores = (probs * (dprobs - delta)).astype(bf16)
            dq2 = lax.dot_general(
                dscores, keys, (((0,), (0,)), ((), ())), preferred_element_type=f32
            )
            dq = jnp.where(first, dq2[0:rows], dq2[rows : 2 * rows]) * scale
            dq_ref[:, cols(tile)] = dq.astype(bf16)
            mid = (((1,), (0,)), ((), ()))
            part[0, tile] = lax.dot_general(dscores, q2, mid, preferred_element_type=f32) * scale
            part[1, tile] = lax.dot_general(low_probs, g2, mid, preferred_element_type=f32)

        def give(c, d):
            at_d = pl.ds(d * rows, rows)
            total = part[:, group(c), at_d, :]
            if d < REACH:
                back(c, d + 1).wait_recv()
                total = total + in_buf[:, group(c), at_d, :].astype(f32)
            out_buf[:, group(c), pl.ds((d - 1) * rows, rows), :] = total.astype(bf16)
            back(c, d).start()

        def settle(c):
            back(c, 1).wait_recv()
            for j in range(GROUP):
                tile = c * GROUP + j
                total = part[:, tile, pl.ds(0, rows), :] + in_buf[:, tile, pl.ds(0, rows), :].astype(f32)
                low_total = total.astype(bf16)
                dk_ref[:, cols(tile)] = low_total[0]
                vg[tile] = low_total[1]
            grads_halo(c).start()

        def finish(tile):
            own = vg[tile].astype(f32)
            ext[0:rows, :] = own
            ext[rows : rows + RIM, :] = v_halo[tile].astype(f32)
            for k in range(8):
                moved[k] = ext[k : k + shifted_rows, :]
            reach = right[...]

            def body(q, total):
                tap_rows = taps_at(q, tile)
                base = pl.multiple_of(8 * q, 8)
                first = (q * 8).astype(f32)
                for k in range(8):
                    piece = moved[k, pl.ds(base, rows), :]
                    total = total + jnp.where(reach >= first + k, piece * tap_rows[k : k + 1, :], 0.0)
                return total

            total = lax.fori_loop(0, taps // 8, body, jnp.zeros((rows, LANES), f32))
            de_ref[:, cols(tile)] = total.astype(bf16)
            load_events(tile)
            reach_l = left[...]

            def tap_body(q, _):
                base = pl.multiple_of(RIM - 8 - 8 * q, 8)
                first = (q * 8).astype(f32)
                sums = []
                for k in range(8):
                    piece = moved[k, pl.ds(base, rows), :]
                    kept = jnp.where(reach_l >= first + k, piece * own, 0.0)
                    sums.append(jnp.sum(kept, axis=0, keepdims=True))
                f_ref[pl.ds(pl.multiple_of(q * 8, 8), 8), cols(tile)] = jnp.concatenate(sums, axis=0)
                return 0

            lax.fori_loop(0, taps // 8, tap_body, 0)

        def finish_chunk(c):
            grads_halo(c).wait_recv()
            for j in range(GROUP):
                finish(c * GROUP + j)

        def early(c, _):
            conv_chunk(c)
            return 0

        lax.fori_loop(0, min(2, chunks), early, 0)
        fwd(0, 1).start()

        def tick(i, _):
            a, b, z = i - 1, i - 2, i - 3
            on_f = i < chunks
            on_a = jnp.logical_and(a >= 0, a < chunks)
            on_b = jnp.logical_and(b >= 0, b < chunks)
            on_z = jnp.logical_and(z >= 0, z < chunks)

            @pl.when(i + 1 < chunks)
            def _():
                fwd(i + 1, 1).start()

            @pl.when(on_z)
            def _():
                settle(z)

            for s in range(REACH):
                @pl.when(on_b)
                def _():
                    give(b, REACH - s)

                @pl.when(on_f)
                def _():
                    fwd(i, s + 1).wait_recv()
                    if s + 1 < REACH:
                        fwd(i, s + 2).start()

                if s < GROUP:
                    @pl.when(on_a)
                    def _():
                        attend(a * GROUP + s)

                if s == 2:
                    @pl.when(i + 2 < chunks)
                    def _():
                        conv_chunk(i + 2)

                if s == 3:
                    @pl.when(on_z)
                    def _():
                        finish_chunk(z)

            return 0

        lax.fori_loop(0, chunks + 3, tick, 0)

        for slot in range(REACH + 1):
            ids_to(slot).wait_send()

        def drain(c, _):
            events_halo(c).wait_send()
            grads_halo(c).wait_send()
            for d in range(1, REACH + 1):
                fwd(c, d).wait_send()
                back(c, d).wait_send()
            return 0

        lax.fori_loop(0, chunks, drain, 0)

    vmem = pl.BlockSpec(memory_space=pltpu.VMEM)
    sems = pltpu.SemaphoreType.DMA
    tall = jax.ShapeDtypeStruct((rows, width), bf16)
    return pl.pallas_call(
        kernel,
        out_shape=(tall, tall, tall, jax.ShapeDtypeStruct((taps, width), f32)),
        in_specs=[vmem] * 7,
        out_specs=(vmem,) * 4,
        scratch_shapes=[
            pltpu.VMEM((2, tiles, span, LANES), bf16),
            pltpu.VMEM((2, tiles, span, LANES), f32),
            pltpu.VMEM((2, tiles, span - rows, LANES), bf16),
            pltpu.VMEM((2, tiles, span - rows, LANES), bf16),
            pltpu.VMEM((tiles, RIM, LANES), bf16),
            pltpu.VMEM((tiles, RIM, LANES), bf16),
            pltpu.VMEM((tiles, rows, LANES), bf16),
            pltpu.VMEM((tiles, RIM, LANES), bf16),
            pltpu.VMEM((8, LANES), f32),
            pltpu.VMEM((REACH + 1, 8, LANES), f32),
            pltpu.VMEM((span, 2 * rows), f32),
            pltpu.VMEM((rows, LANES), f32),
            pltpu.VMEM((rows, LANES), f32),
            pltpu.VMEM((rows + RIM, LANES), f32),
            pltpu.VMEM((8, shifted_rows, LANES), f32),
            sems((chunks, REACH)), sems((chunks, REACH)),
            sems((chunks, REACH)), sems((chunks, REACH)),
            sems((chunks,)), sems((chunks,)), sems((chunks,)), sems((chunks,)),
            sems((REACH + 1,)), sems((REACH + 1,)),
        ],
        compiler_params=pltpu.CompilerParams(
            collective_id=0, has_side_effects=True, vmem_limit_bytes=48 * 1024 * 1024
        ),
        name="timeline",
    )(query, key_rows, feats, grad, ids, picked, weight)


def per_device(queries, keys, events, out_grad, segment_ids, block_list, conv_weight):
    blist = block_list[0]
    shards = lax.axis_size("dp") * lax.axis_size("seq")
    here = lax.axis_index("seq")
    own = lax.dynamic_slice_in_dim(blist, here, 1, 0)
    wanted = here - jnp.arange(8, dtype=jnp.int32)
    hit = jnp.any(own == wanted[:, None], axis=1) & (wanted >= 0)
    picked = jnp.broadcast_to(hit.astype(jnp.float32)[:, None], (8, LANES))
    q_grad, k_grad, e_grad, f_local = timeline(
        queries[0], keys[0], events[0], out_grad[0], segment_ids, picked, conv_weight
    )
    f_grad = spread_sum(f_local, 1.0 / shards)
    return (q_grad[None], k_grad[None], e_grad[None], f_grad)


def solution(mesh):
    in_specs = (
        P("dp", "seq", None),
        P("dp", "seq", None),
        P("dp", "seq", None),
        P("dp", "seq", None),
        P("dp", "seq"),
        P("dp", None, None),
        P(),
    )
    out_specs = (P("dp", "seq", None), P("dp", "seq", None), P("dp", "seq", None), P())
    return jax.shard_map(
        per_device, mesh=mesh, in_specs=in_specs, out_specs=out_specs, check_vma=False
    )
```

```python
import jax
import jax.numpy as jnp
from jax import lax
from jax.experimental import pallas as pl
from jax.experimental.pallas import tpu as pltpu
from jax.sharding import PartitionSpec as P

HD = 64
REACH = 4
LANES = 128
RIM = 64
BATCH = 4
MESH = pl.DeviceIdType.MESH


def timeline(query, key_rows, feats, grad, ids, picked, weight):
    n_dp, n_seq = lax.axis_size("dp"), lax.axis_size("seq")
    rows, width = query.shape
    taps = weight.shape[0]
    tiles = width // LANES
    batch = min(BATCH, tiles)
    split = n_dp // tiles
    piece = taps // split
    mean = 1.0 / (n_dp * n_seq)
    scale = HD ** (-0.5)
    span = (REACH + 1) * rows
    shifted_rows = rows + RIM - 8
    f32, bf16 = jnp.float32, jnp.bfloat16

    def kernel(
        q_in, k_in, e_in, g_in, id_ref, pick_ref, w_in,
        dq_ref, dk_ref, de_ref, f_out,
        win, part, out_buf, in_buf, e_halo, v_halo, vg, e_src,
        id_src, id_buf, cap, left, right, ext, moved,
        q_ref, k_ref, e_ref, g_ref, w_ref, load_s,
        f_ref, mine, got, part_sum, got_z, total_sum, whole, sum_s, sum_r,
        win_s, win_r, back_s, back_r, eh_s, eh_r, vh_s, vh_r, id_s, id_r,
    ):
        me, lane_me = lax.axis_index("seq"), lax.axis_index("dp")

        def at(offset):
            return lax.rem(me + offset + n_seq, n_seq)

        up, down = at(1), at(-1)

        def remote(src, dst, send, recv, to):
            return pltpu.make_async_remote_copy(
                src_ref=src, dst_ref=dst, send_sem=send, recv_sem=recv,
                device_id={"seq": to}, device_id_type=MESH,
            )

        def cols(tile):
            return pl.ds(pl.multiple_of(tile * LANES, LANES), LANES)

        def fwd(t, d):
            return remote(
                win.at[:, t, pl.ds((d - 1) * rows, rows), :],
                win.at[:, t, pl.ds(d * rows, rows), :],
                win_s.at[t, d - 1], win_r.at[t, d - 1], up,
            )

        def back(t, d):
            return remote(
                out_buf.at[:, t, pl.ds((d - 1) * rows, rows), :],
                in_buf.at[:, t, pl.ds((d - 1) * rows, rows), :],
                back_s.at[t, d - 1], back_r.at[t, d - 1], down,
            )

        def events_halo(n):
            several = pl.ds(n * batch, batch)
            return remote(e_src.at[several], e_halo.at[several], eh_s.at[n], eh_r.at[n], up)

        def grads_halo(t):
            return remote(
                vg.at[t, pl.ds(0, RIM), :], v_halo.at[t], vh_s.at[t], vh_r.at[t], down
            )

        def ids_to(slot):
            to = down if slot == 0 else at(slot)
            return remote(id_src, id_buf.at[slot], id_s.at[slot], id_r.at[slot], to)

        loads = [
            pltpu.make_async_copy(src, dst, load_s.at[n])
            for n, (src, dst) in enumerate(
                ((e_in, e_ref), (k_in, k_ref), (w_in, w_ref), (q_in, q_ref), (g_in, g_ref))
            )
        ]
        for load in loads:
            load.start()
        barrier = pltpu.get_barrier_semaphore()

        def greet_seq(n, _):
            pl.semaphore_signal(barrier, inc=1, device_id={"seq": at(n)}, device_id_type=MESH)
            return 0

        def greet_dp(n, _):
            to = lax.rem(lane_me + n, n_dp)
            pl.semaphore_signal(barrier, inc=1, device_id={"dp": to}, device_id_type=MESH)
            return 0

        lax.fori_loop(1, n_seq, greet_seq, 0)
        lax.fori_loop(1, n_dp, greet_dp, 0)
        own_ids = id_ref[...].astype(f32)
        id_src[...] = jnp.broadcast_to(own_ids, id_src.shape)

        for load in loads:
            load.wait()

        def stage(tile, _):
            win[0, tile, pl.ds(0, rows), :] = k_ref[:, cols(tile)]
            e_src[tile] = e_ref[pl.ds(rows - RIM, RIM), cols(tile)]
            return 0

        lax.fori_loop(0, tiles, stage, 0)
        pl.semaphore_wait(barrier, n_seq + n_dp - 2)
        for slot in range(REACH + 1):
            ids_to(slot).start()

        def start_halo(c, _):
            events_halo(c).start()
            return 0

        lax.fori_loop(0, tiles // batch, start_halo, 0)
        for slot in range(REACH + 1):
            ids_to(slot).wait_recv()

        square = (rows, rows)
        own_row = jnp.broadcast_to(own_ids, square)

        def same(row):
            col = jnp.broadcast_to(row, square).T
            return jnp.where(col == own_row, 1.0, 0.0)

        s_at = lax.broadcasted_iota(jnp.int32, square, 0)
        r_at = lax.broadcasted_iota(jnp.int32, square, 1)
        here = same(own_ids)
        low = jnp.where(s_at <= r_at, here, 0.0)
        high = jnp.where(s_at >= r_at, here, 0.0)
        before = same(id_buf[1][0:1]) * jnp.where(me > 0, 1.0, 0.0)
        after = same(id_buf[0][0:1]) * jnp.where(me < n_seq - 1, 1.0, 0.0)
        reach_left = jnp.sum(low, axis=0, keepdims=True) + jnp.sum(before, axis=0, keepdims=True) - 1.0
        reach_right = jnp.sum(high, axis=0, keepdims=True) + jnp.sum(after, axis=0, keepdims=True) - 1.0
        left[...] = jnp.broadcast_to(reach_left, square).T
        right[...] = jnp.broadcast_to(reach_right, square).T
        for d in range(REACH + 1):
            open_pairs = low if d == 0 else same(id_buf[d][0:1])
            open_pairs = open_pairs * jnp.broadcast_to(pick_ref[d : d + 1, :], square)
            limit = jnp.where(open_pairs > 0.5, 3.0e38, -1.0e30)
            cap[d * rows : (d + 1) * rows, 0:rows] = limit
            cap[d * rows : (d + 1) * rows, rows : 2 * rows] = limit

        def shift_back():
            for k in range(8):
                moved[k] = ext[8 - k : 8 - k + shifted_rows, :]

        def load_events(tile):
            ext[0:RIM, :] = e_halo[tile].astype(f32)
            ext[RIM : RIM + rows, :] = e_ref[:, cols(tile)].astype(f32)
            shift_back()

        def taps_at(q, tile):
            return w_ref[pl.ds(pl.multiple_of(q * 8, 8), 8), cols(tile)]

        def conv(tile):
            load_events(tile)
            reach = left[...]

            def body(q, total):
                tap_rows = taps_at(q, tile)
                base = pl.multiple_of(RIM - 8 - 8 * q, 8)
                first = (q * 8).astype(f32)
                for k in range(8):
                    piece = moved[k, pl.ds(base, rows), :]
                    total = total + jnp.where(reach >= first + k, piece * tap_rows[k : k + 1, :], 0.0)
                return total

            total = lax.fori_loop(0, taps // 8, body, jnp.zeros((rows, LANES), f32))
            win[1, tile, pl.ds(0, rows), :] = total.astype(bf16)

        def conv_next(tile):
            @pl.when(lax.rem(tile, batch) == 0)
            def _():
                events_halo(tile // batch).wait_recv()

            conv(tile)

        def attend(tile):
            lane = lax.broadcasted_iota(jnp.int32, (rows, LANES), 1)
            first = lane < HD

            def pair(ref):
                both = ref[:, cols(tile)].astype(f32)
                return jnp.concatenate(
                    [jnp.where(first, both, 0.0), jnp.where(first, 0.0, both)], axis=0
                ).astype(bf16)

            q2, g2 = pair(q_ref), pair(g_ref)
            keys, vals = win[0, tile], win[1, tile]
            last = (((1,), (1,)), ((), ()))
            scores = lax.dot_general(keys, q2, last, preferred_element_type=f32)
            scores = jnp.minimum(scores * scale, cap[...])
            top = jnp.max(scores, axis=0, keepdims=True)
            raw = jnp.exp(scores - top)
            probs = raw * (1.0 / jnp.sum(raw, axis=0, keepdims=True))
            low_probs = probs.astype(bf16)
            dprobs = lax.dot_general(vals, g2, last, preferred_element_type=f32)
            delta = jnp.sum(low_probs.astype(f32) * dprobs, axis=0, keepdims=True)
            dscores = (probs * (dprobs - delta)).astype(bf16)
            dq2 = lax.dot_general(
                dscores, keys, (((0,), (0,)), ((), ())), preferred_element_type=f32
            )
            dq = jnp.where(first, dq2[0:rows], dq2[rows : 2 * rows]) * scale
            dq_ref[:, cols(tile)] = dq.astype(bf16)
            mid = (((1,), (0,)), ((), ()))
            part[0, tile] = lax.dot_general(dscores, q2, mid, preferred_element_type=f32) * scale
            part[1, tile] = lax.dot_general(low_probs, g2, mid, preferred_element_type=f32)

        def give(t, d):
            at_d = pl.ds(d * rows, rows)
            total = part[:, t, at_d, :]
            if d < REACH:
                back(t, d + 1).wait_recv()
                total = total + in_buf[:, t, at_d, :].astype(f32)
            out_buf[:, t, pl.ds((d - 1) * rows, rows), :] = total.astype(bf16)
            back(t, d).start()

        def settle(t):
            back(t, 1).wait_recv()
            total = part[:, t, pl.ds(0, rows), :] + in_buf[:, t, pl.ds(0, rows), :].astype(f32)
            low_total = total.astype(bf16)
            dk_ref[:, cols(t)] = low_total[0]
            vg[t] = low_total[1]
            grads_halo(t).start()

        def events_back(tile):
            grads_halo(tile).wait_recv()
            own = vg[tile].astype(f32)
            ext[0:rows, :] = own
            ext[rows : rows + RIM, :] = v_halo[tile].astype(f32)
            for k in range(8):
                moved[k] = ext[k : k + shifted_rows, :]
            reach = right[...]

            def body(q, total):
                tap_rows = taps_at(q, tile)
                base = pl.multiple_of(8 * q, 8)
                first = (q * 8).astype(f32)
                for k in range(8):
                    piece = moved[k, pl.ds(base, rows), :]
                    total = total + jnp.where(reach >= first + k, piece * tap_rows[k : k + 1, :], 0.0)
                return total

            total = lax.fori_loop(0, taps // 8, body, jnp.zeros((rows, LANES), f32))
            de_ref[:, cols(tile)] = total.astype(bf16)

        def tap_sums(tile):
            own = vg[tile].astype(f32)
            load_events(tile)
            reach_l = left[...]

            def tap_body(q, _):
                base = pl.multiple_of(RIM - 8 - 8 * q, 8)
                first = (q * 8).astype(f32)
                sums = []
                for k in range(8):
                    piece = moved[k, pl.ds(base, rows), :]
                    kept = jnp.where(reach_l >= first + k, piece * own, 0.0)
                    sums.append(jnp.sum(kept, axis=0, keepdims=True))
                f_ref[pl.ds(pl.multiple_of(q * 8, 8), 8), :] = jnp.concatenate(sums, axis=0)
                return 0

            lax.fori_loop(0, taps // 8, tap_body, 0)
            share(tile)

        def to_dp(src, dst, n, to):
            return pltpu.make_async_remote_copy(
                src_ref=src, dst_ref=dst, send_sem=sum_s.at[n], recv_sem=sum_r.at[n],
                device_id={"dp": to}, device_id_type=MESH,
            )

        def share(tile):
            for h in range(split):
                owner = tile * split + h
                mine[owner] = f_ref[h * piece : (h + 1) * piece, :].astype(bf16)

                @pl.when(owner == lane_me)
                def _():
                    got[owner] = mine[owner]

                @pl.when(owner != lane_me)
                def _():
                    to_dp(mine.at[owner], got.at[lane_me], 0, owner).start()

        def settled(ref, n, count):
            pltpu.make_async_copy(ref.at[pl.ds(0, count)], ref.at[pl.ds(0, count)], n).wait()

        def sum_all():
            settled(got, sum_r.at[0], n_dp - 1)
            total = got[0].astype(f32)
            for n in range(1, n_dp):
                total = total + got[n].astype(f32)
            part_sum[...] = total.astype(bf16)

            def send_z(n, _):
                remote(part_sum, got_z.at[me], sum_s.at[1], sum_r.at[1], at(n)).start()
                return 0

            lax.fori_loop(1, n_seq, send_z, 0)
            got_z[me] = part_sum[...]
            settled(got_z, sum_r.at[1], n_seq - 1)
            total = got_z[0].astype(f32)
            for n in range(1, n_seq):
                total = total + got_z[n].astype(f32)
            total_sum[...] = (total * mean).astype(bf16)

            def send_dp(n, _):
                to_dp(total_sum, whole.at[lane_me], 2, lax.rem(lane_me + n, n_dp)).start()
                return 0

            lax.fori_loop(1, n_dp, send_dp, 0)
            whole[lane_me] = total_sum[...]
            settled(whole, sum_r.at[2], n_dp - 1)
            for n in range(n_dp):
                col, row = (n // split) * LANES, (n % split) * piece
                f_out[row : row + piece, col : col + LANES] = whole[n].astype(f32)
            settled(mine, sum_s.at[0], n_dp - 1)
            settled(got_z, sum_s.at[1], n_seq - 1)
            settled(whole, sum_s.at[2], n_dp - 1)

        conv_next(0)
        conv_next(1)

        def tick(i, _):
            def on(t, act):
                @pl.when(jnp.logical_and(t >= 0, t < tiles))
                def _():
                    act(t)

            def pass_on(t, d):
                fwd(t, d - 1).wait_recv()
                fwd(t, d).start()

            def meet(t):
                fwd(t, REACH).wait_recv()
                attend(t)

            on(i, lambda t: fwd(t, 1).start())
            on(i - 5, lambda t: give(t, 4))
            on(i - 1, lambda t: pass_on(t, 2))
            on(i - 6, lambda t: give(t, 3))

            @pl.when(i + 2 < tiles)
            def _():
                conv_next(i + 2)

            on(i - 2, lambda t: pass_on(t, 3))
            on(i - 7, lambda t: give(t, 2))
            on(i - 10, events_back)
            on(i - 3, lambda t: pass_on(t, 4))
            on(i - 8, lambda t: give(t, 1))
            on(i - 10, tap_sums)
            on(i - 9, settle)
            on(i - 4, meet)
            return 0

        lax.fori_loop(0, tiles + 10, tick, 0)

        sum_all()
        for slot in range(REACH + 1):
            ids_to(slot).wait_send()

        def drain(t, _):
            grads_halo(t).wait_send()
            for d in range(1, REACH + 1):
                fwd(t, d).wait_send()
                back(t, d).wait_send()
            return 0

        def drain_halo(n, _):
            events_halo(n).wait_send()
            return 0

        lax.fori_loop(0, tiles, drain, 0)
        lax.fori_loop(0, tiles // batch, drain_halo, 0)

    vmem = pl.BlockSpec(memory_space=pltpu.VMEM)
    hbm = pl.BlockSpec(memory_space=pl.ANY)
    sems = pltpu.SemaphoreType.DMA
    tall = jax.ShapeDtypeStruct((rows, width), bf16)
    return pl.pallas_call(
        kernel,
        out_shape=(tall, tall, tall, jax.ShapeDtypeStruct((taps, width), f32)),
        in_specs=[hbm] * 4 + [vmem, vmem, hbm],
        out_specs=(vmem,) * 4,
        scratch_shapes=[
            pltpu.VMEM((2, tiles, span, LANES), bf16),
            pltpu.VMEM((2, tiles, span, LANES), f32),
            pltpu.VMEM((2, tiles, span - rows, LANES), bf16),
            pltpu.VMEM((2, tiles, span - rows, LANES), bf16),
            pltpu.VMEM((tiles, RIM, LANES), bf16),
            pltpu.VMEM((tiles, RIM, LANES), bf16),
            pltpu.VMEM((tiles, rows, LANES), bf16),
            pltpu.VMEM((tiles, RIM, LANES), bf16),
            pltpu.VMEM((8, LANES), f32),
            pltpu.VMEM((REACH + 1, 8, LANES), f32),
            pltpu.VMEM((span, 2 * rows), f32),
            pltpu.VMEM((rows, LANES), f32),
            pltpu.VMEM((rows, LANES), f32),
            pltpu.VMEM((rows + RIM, LANES), f32),
            pltpu.VMEM((8, shifted_rows, LANES), f32),
            *[pltpu.VMEM((rows, width), bf16)] * 4,
            pltpu.VMEM((taps, width), f32),
            sems((5,)),
            pltpu.VMEM((taps, LANES), f32),
            pltpu.VMEM((n_dp, piece, LANES), bf16),
            pltpu.VMEM((n_dp, piece, LANES), bf16),
            pltpu.VMEM((piece, LANES), bf16),
            pltpu.VMEM((n_seq, piece, LANES), bf16),
            pltpu.VMEM((piece, LANES), bf16),
            pltpu.VMEM((n_dp, piece, LANES), bf16),
            sems((3,)), sems((3,)),
            sems((tiles, REACH)), sems((tiles, REACH)),
            sems((tiles, REACH)), sems((tiles, REACH)),
            sems((tiles // batch,)), sems((tiles // batch,)), sems((tiles,)), sems((tiles,)),
            sems((REACH + 1,)), sems((REACH + 1,)),
        ],
        compiler_params=pltpu.CompilerParams(
            collective_id=0, has_side_effects=True, vmem_limit_bytes=48 * 1024 * 1024
        ),
        name="timeline",
    )(query, key_rows, feats, grad, ids, picked, weight)


def per_device(queries, keys, events, out_grad, segment_ids, block_list, conv_weight):
    blist = block_list[0]
    here = lax.axis_index("seq")
    own = lax.dynamic_slice_in_dim(blist, here, 1, 0)
    wanted = here - jnp.arange(8, dtype=jnp.int32)
    hit = jnp.any(own == wanted[:, None], axis=1) & (wanted >= 0)
    picked = jnp.broadcast_to(hit.astype(jnp.float32)[:, None], (8, LANES))
    q_grad, k_grad, e_grad, f_grad = timeline(
        queries[0], keys[0], events[0], out_grad[0], segment_ids, picked, conv_weight
    )
    return (q_grad[None], k_grad[None], e_grad[None], f_grad)


def solution(mesh):
    in_specs = (
        P("dp", "seq", None),
        P("dp", "seq", None),
        P("dp", "seq", None),
        P("dp", "seq", None),
        P("dp", "seq"),
        P("dp", None, None),
        P(),
    )
    out_specs = (P("dp", "seq", None), P("dp", "seq", None), P("dp", "seq", None), P())
    return jax.shard_map(
        per_device, mesh=mesh, in_specs=in_specs, out_specs=out_specs, check_vma=False
    )
```

```python
import jax
import jax.numpy as jnp
from jax import lax
from jax.experimental import pallas as pl
from jax.experimental.pallas import tpu as pltpu
from jax.sharding import PartitionSpec as P

HD = 64
REACH = 4
LANES = 128
RIM = 64
BATCH = 4
PAIR = 2
QUAD = 4
MESH = pl.DeviceIdType.MESH


def timeline(query, key_rows, feats, grad, ids, picked, weight):
    n_dp, n_seq = lax.axis_size("dp"), lax.axis_size("seq")
    rows, width = query.shape
    taps = weight.shape[0]
    tiles = width // LANES
    batch = min(BATCH, tiles)
    half = tiles // PAIR
    units = 2 * half
    conv_lag = min(2, half - 1)
    rounds = n_seq // QUAD
    split = n_dp // tiles
    piece = taps // split
    mean = 1.0 / (n_dp * n_seq)
    scale = HD ** (-0.5)
    span = (REACH + 1) * rows
    shifted_rows = rows + RIM - 8
    f32, bf16 = jnp.float32, jnp.bfloat16

    def kernel(
        q_in, k_in, e_in, g_in, id_ref, pick_ref, w_in,
        dq_ref, dk_ref, de_ref, f_out,
        win, part, out_buf, in_buf, e_halo, v_halo, vg, e_src,
        id_src, id_buf, cap, left, right, ext, moved,
        q_ref, k_ref, e_ref, g_ref, w_ref, load_s,
        probs_ref, f_ref, mine, got, near, far, near_in, far_in, total_sum, whole, sum_s, sum_r,
        win_s, win_r, back_s, back_r, eh_s, eh_r, vh_s, vh_r, id_s, id_r,
    ):
        me, lane_me = lax.axis_index("seq"), lax.axis_index("dp")

        def at(offset):
            return lax.rem(me + offset + n_seq, n_seq)

        up, down = at(1), at(-1)

        def remote(src, dst, send, recv, to):
            return pltpu.make_async_remote_copy(
                src_ref=src, dst_ref=dst, send_sem=send, recv_sem=recv,
                device_id={"seq": to}, device_id_type=MESH,
            )

        def cols(tile):
            return pl.ds(pl.multiple_of(tile * LANES, LANES), LANES)

        def both(u):
            return pl.ds(u * PAIR, PAIR)

        def fwd(u, d):
            return remote(
                win.at[both(u), pl.ds((d - 1) * rows, rows), :],
                win.at[both(u), pl.ds(d * rows, rows), :],
                win_s.at[u, d - 1], win_r.at[u, d - 1], up,
            )

        def back(u, d):
            return remote(
                out_buf.at[both(u), pl.ds((d - 1) * rows, rows), :],
                in_buf.at[both(u), pl.ds((d - 1) * rows, rows), :],
                back_s.at[u, d - 1], back_r.at[u, d - 1], down,
            )

        def events_halo(n):
            several = pl.ds(n * batch, batch)
            return remote(e_src.at[several], e_halo.at[several], eh_s.at[n], eh_r.at[n], up)

        def grads_halo(u):
            return remote(
                vg.at[both(u), pl.ds(0, RIM), :], v_halo.at[both(u)], vh_s.at[u], vh_r.at[u], down
            )

        def ids_to(slot):
            to = down if slot == 0 else at(slot)
            return remote(id_src, id_buf.at[slot], id_s.at[slot], id_r.at[slot], to)

        loads = [
            pltpu.make_async_copy(src, dst, load_s.at[n])
            for n, (src, dst) in enumerate(
                ((e_in, e_ref), (k_in, k_ref), (w_in, w_ref), (q_in, q_ref), (g_in, g_ref))
            )
        ]
        for load in loads:
            load.start()
        barrier = pltpu.get_barrier_semaphore()

        def greet_seq(n, _):
            pl.semaphore_signal(barrier, inc=1, device_id={"seq": at(n)}, device_id_type=MESH)
            return 0

        def greet_dp(n, _):
            to = lax.rem(lane_me + n, n_dp)
            pl.semaphore_signal(barrier, inc=1, device_id={"dp": to}, device_id_type=MESH)
            return 0

        lax.fori_loop(1, n_seq, greet_seq, 0)
        lax.fori_loop(1, n_dp, greet_dp, 0)
        own_ids = id_ref[...].astype(f32)
        id_src[...] = jnp.broadcast_to(own_ids, id_src.shape)

        for load in loads:
            load.wait()

        def stage(tile, _):
            win[tile, pl.ds(0, rows), :] = k_ref[:, cols(tile)]
            e_src[tile] = e_ref[pl.ds(rows - RIM, RIM), cols(tile)]
            return 0

        lax.fori_loop(0, tiles, stage, 0)
        pl.semaphore_wait(barrier, n_seq + n_dp - 2)
        for slot in range(REACH + 1):
            ids_to(slot).start()

        fwd(0, 1).start()
        for slot in range(REACH + 1):
            ids_to(slot).wait_recv()

        square = (rows, rows)
        own_row = jnp.broadcast_to(own_ids, square)

        def same(row):
            col = jnp.broadcast_to(row, square).T
            return jnp.where(col == own_row, 1.0, 0.0)

        s_at = lax.broadcasted_iota(jnp.int32, square, 0)
        r_at = lax.broadcasted_iota(jnp.int32, square, 1)
        here = same(own_ids)
        low = jnp.where(s_at <= r_at, here, 0.0)
        high = jnp.where(s_at >= r_at, here, 0.0)
        before = same(id_buf[1][0:1]) * jnp.where(me > 0, 1.0, 0.0)
        after = same(id_buf[0][0:1]) * jnp.where(me < n_seq - 1, 1.0, 0.0)
        reach_left = jnp.sum(low, axis=0, keepdims=True) + jnp.sum(before, axis=0, keepdims=True) - 1.0
        reach_right = jnp.sum(high, axis=0, keepdims=True) + jnp.sum(after, axis=0, keepdims=True) - 1.0
        left[...] = jnp.broadcast_to(reach_left, square).T
        right[...] = jnp.broadcast_to(reach_right, square).T
        for d in range(REACH + 1):
            open_pairs = low if d == 0 else same(id_buf[d][0:1])
            open_pairs = open_pairs * jnp.broadcast_to(pick_ref[d : d + 1, :], square)
            limit = jnp.where(open_pairs > 0.5, 3.0e38, -1.0e30)
            cap[d * rows : (d + 1) * rows, 0:rows] = limit
            cap[d * rows : (d + 1) * rows, rows : 2 * rows] = limit

        def shift_back():
            for k in range(8):
                moved[k] = ext[8 - k : 8 - k + shifted_rows, :]

        def load_events(tile):
            ext[0:RIM, :] = e_halo[tile].astype(f32)
            ext[RIM : RIM + rows, :] = e_ref[:, cols(tile)].astype(f32)
            shift_back()

        def taps_at(q, tile):
            return w_ref[pl.ds(pl.multiple_of(q * 8, 8), 8), cols(tile)]

        def conv(tile):
            load_events(tile)
            reach = left[...]

            def body(q, total):
                tap_rows = taps_at(q, tile)
                base = pl.multiple_of(RIM - 8 - 8 * q, 8)
                first = (q * 8).astype(f32)
                for k in range(8):
                    piece = moved[k, pl.ds(base, rows), :]
                    total = total + jnp.where(reach >= first + k, piece * tap_rows[k : k + 1, :], 0.0)
                return total

            total = lax.fori_loop(0, taps // 8, body, jnp.zeros((rows, LANES), f32))
            win[tiles + tile, pl.ds(0, rows), :] = total.astype(bf16)

        def conv_next(tile):
            @pl.when(lax.rem(tile, batch) == 0)
            def _():
                events_halo(tile // batch).wait_recv()

            conv(tile)

        lane = lax.broadcasted_iota(jnp.int32, (rows, LANES), 1)
        first_head = lane < HD
        last = (((1,), (1,)), ((), ()))
        mid = (((1,), (0,)), ((), ()))

        def heads(ref, tile):
            wide = ref[:, cols(tile)].astype(f32)
            return jnp.concatenate(
                [jnp.where(first_head, wide, 0.0), jnp.where(first_head, 0.0, wide)], axis=0
            ).astype(bf16)

        def attend_keys(tile):
            scores = lax.dot_general(win[tile], heads(q_ref, tile), last, preferred_element_type=f32)
            scores = jnp.minimum(scores * scale, cap[...])
            top = jnp.max(scores, axis=0, keepdims=True)
            raw = jnp.exp(scores - top)
            probs = raw * (1.0 / jnp.sum(raw, axis=0, keepdims=True))
            probs_ref[tile] = probs
            part[tile] = lax.dot_general(
                probs.astype(bf16), heads(g_ref, tile), mid, preferred_element_type=f32
            )

        def attend_values(tile):
            keys, vals = win[tile], win[tiles + tile]
            probs = probs_ref[tile]
            dprobs = lax.dot_general(vals, heads(g_ref, tile), last, preferred_element_type=f32)
            low_probs = probs.astype(bf16).astype(f32)
            delta = jnp.sum(low_probs * dprobs, axis=0, keepdims=True)
            dscores = (probs * (dprobs - delta)).astype(bf16)
            part[tiles + tile] = scale * lax.dot_general(
                dscores, heads(q_ref, tile), mid, preferred_element_type=f32
            )
            dq2 = lax.dot_general(
                dscores, keys, (((0,), (0,)), ((), ())), preferred_element_type=f32
            )
            dq = jnp.where(first_head, dq2[0:rows], dq2[rows : 2 * rows]) * scale
            dq_ref[:, cols(tile)] = dq.astype(bf16)

        def give(u, d):
            at_d = pl.ds(d * rows, rows)
            total = part[both(u), at_d, :]
            if d < REACH:
                back(u, d + 1).wait_recv()
                total = total + in_buf[both(u), at_d, :].astype(f32)
            out_buf[both(u), pl.ds((d - 1) * rows, rows), :] = total.astype(bf16)
            back(u, d).start()

        def settle(u):
            back(u, 1).wait_recv()
            total = part[both(u), pl.ds(0, rows), :] + in_buf[both(u), pl.ds(0, rows), :].astype(f32)
            return total.astype(bf16)

        def settle_values(u):
            vg[both(u)] = settle(u)
            grads_halo(u).start()

        def settle_keys(u):
            low_total = settle(u)
            for n in range(PAIR):
                dk_ref[:, cols((u - half) * PAIR + n)] = low_total[n]

        def events_back(tile):
            own = vg[tile].astype(f32)
            ext[0:rows, :] = own
            ext[rows : rows + RIM, :] = v_halo[tile].astype(f32)
            for k in range(8):
                moved[k] = ext[k : k + shifted_rows, :]
            reach = right[...]

            def body(q, total):
                tap_rows = taps_at(q, tile)
                base = pl.multiple_of(8 * q, 8)
                first = (q * 8).astype(f32)
                for k in range(8):
                    piece = moved[k, pl.ds(base, rows), :]
                    total = total + jnp.where(reach >= first + k, piece * tap_rows[k : k + 1, :], 0.0)
                return total

            total = lax.fori_loop(0, taps // 8, body, jnp.zeros((rows, LANES), f32))
            de_ref[:, cols(tile)] = total.astype(bf16)

        def tap_sums(tile):
            own = vg[tile].astype(f32)
            load_events(tile)
            reach_l = left[...]

            def tap_body(q, _):
                base = pl.multiple_of(RIM - 8 - 8 * q, 8)
                first = (q * 8).astype(f32)
                sums = []
                for k in range(8):
                    piece = moved[k, pl.ds(base, rows), :]
                    kept = jnp.where(reach_l >= first + k, piece * own, 0.0)
                    sums.append(jnp.sum(kept, axis=0, keepdims=True))
                f_ref[pl.ds(pl.multiple_of(q * 8, 8), 8), :] = jnp.concatenate(sums, axis=0)
                return 0

            lax.fori_loop(0, taps // 8, tap_body, 0)
            share(tile)

        def to_dp(src, dst, n, to):
            return pltpu.make_async_remote_copy(
                src_ref=src, dst_ref=dst, send_sem=sum_s.at[n], recv_sem=sum_r.at[n],
                device_id={"dp": to}, device_id_type=MESH,
            )

        def share(tile):
            for h in range(split):
                owner = tile * split + h
                mine[owner] = f_ref[h * piece : (h + 1) * piece, :].astype(bf16)

                @pl.when(owner == lane_me)
                def _():
                    got[owner] = mine[owner]

                @pl.when(owner != lane_me)
                def _():
                    to_dp(mine.at[owner], got.at[lane_me], 0, owner).start()

        def settled(ref, n, count):
            pltpu.make_async_copy(ref.at[pl.ds(0, count)], ref.at[pl.ds(0, count)], n).wait()

        my_quad, my_place = lax.div(me, QUAD), lax.rem(me, QUAD)

        def added(ref, count):
            total = ref[0].astype(f32)
            for n in range(1, count):
                total = total + ref[n].astype(f32)
            return total

        def sum_near():
            settled(got, sum_r.at[0], n_dp - 1)
            near[...] = added(got, n_dp).astype(bf16)
            near_in[my_place] = near[...]
            for n in range(1, QUAD):
                to = my_quad * QUAD + lax.rem(my_place + n, QUAD)
                remote(near, near_in.at[my_place], sum_s.at[1], sum_r.at[1], to).start()

        def sum_far():
            settled(near_in, sum_r.at[1], QUAD - 1)
            far[...] = added(near_in, QUAD).astype(bf16)
            far_in[my_quad] = far[...]
            for n in range(1, rounds):
                remote(far, far_in.at[my_quad], sum_s.at[2], sum_r.at[2], at(n * QUAD)).start()

        def send_dp(n, _):
            to_dp(total_sum, whole.at[lane_me], 3, lax.rem(lane_me + n, n_dp)).start()
            return 0

        def sum_out():
            settled(far_in, sum_r.at[2], rounds - 1)
            total_sum[...] = (added(far_in, rounds) * mean).astype(bf16)
            whole[lane_me] = total_sum[...]
            lax.fori_loop(1, n_dp // 2, send_dp, 0)

        def sum_end():
            settled(whole, sum_r.at[3], n_dp - 1)
            for n in range(n_dp):
                col, row = (n // split) * LANES, (n % split) * piece
                f_out[row : row + piece, col : col + LANES] = whole[n].astype(f32)
            settled(mine, sum_s.at[0], n_dp - 1)
            settled(near_in, sum_s.at[1], QUAD - 1)
            settled(far_in, sum_s.at[2], rounds - 1)
            settled(whole, sum_s.at[3], n_dp - 1)

        def each(act, first):
            def body(n, _):
                act(first + n)
                return 0

            lax.fori_loop(0, PAIR, body, 0)

        def meet_keys(u):
            fwd(u, REACH).wait_recv()
            for n in range(PAIR):
                attend_keys(u * PAIR + n)

        def meet_values(u):
            fwd(u, REACH).wait_recv()
            for n in range(PAIR):
                attend_values((u - half) * PAIR + n)

        def values_done(u):
            settle_values(u)
            each(tap_sums, u * PAIR)

        def events_pair(u):
            grads_halo(u).wait_recv()
            each(events_back, u * PAIR)

        def pass_on(u, d):
            fwd(u, d - 1).wait_recv()
            fwd(u, d).start()

        summed = half + 8

        def tick(i, _):
            def on(u, act, low_end=0, high_end=units):
                @pl.when(jnp.logical_and(u >= low_end, u < high_end))
                def _():
                    act(u)

            on(i, lambda u: fwd(u, 1).start(), low_end=1)
            on(i, lambda n: events_halo(n).start(), high_end=tiles // batch)
            on(i - 5, lambda u: give(u, 4))
            on(i - 1, lambda u: pass_on(u, 2))
            on(i - 6, lambda u: give(u, 3))
            on(i - conv_lag, lambda p: each(conv_next, p * PAIR), high_end=half)
            on(i - 2, lambda u: pass_on(u, 3))
            on(i - 7, lambda u: give(u, 2))
            on(i - 10, events_pair, high_end=half)
            on(i - 3, lambda u: pass_on(u, 4))
            on(i - 8, lambda u: give(u, 1))
            on(i - 9, values_done, high_end=half)
            on(i - 9, settle_keys, low_end=half)
            pl.when(i == summed + 2)(sum_near)
            pl.when(i == summed + 3)(sum_far)
            pl.when(i == summed + 5)(sum_out)

            @pl.when(i == summed + 6)
            def _():
                lax.fori_loop(n_dp // 2, n_dp, send_dp, 0)

            on(i - 4, meet_keys, high_end=half)
            on(i - 4, meet_values, low_end=half)
            return 0

        lax.fori_loop(0, max(units + 9, summed + 7), tick, 0)
        sum_end()
        for slot in range(REACH + 1):
            ids_to(slot).wait_send()

        def drain(u, _):
            for d in range(1, REACH + 1):
                fwd(u, d).wait_send()
                back(u, d).wait_send()
            return 0

        def drain_grads(u, _):
            grads_halo(u).wait_send()
            return 0

        def drain_halo(n, _):
            events_halo(n).wait_send()
            return 0

        lax.fori_loop(0, units, drain, 0)
        lax.fori_loop(0, half, drain_grads, 0)
        lax.fori_loop(0, tiles // batch, drain_halo, 0)

    vmem = pl.BlockSpec(memory_space=pltpu.VMEM)
    hbm = pl.BlockSpec(memory_space=pltpu.HBM)
    sems = pltpu.SemaphoreType.DMA
    tall = jax.ShapeDtypeStruct((rows, width), bf16)
    return pl.pallas_call(
        kernel,
        out_shape=(tall, tall, tall, jax.ShapeDtypeStruct((taps, width), f32)),
        in_specs=[hbm] * 4 + [vmem, vmem, hbm],
        out_specs=(vmem,) * 4,
        scratch_shapes=[
            pltpu.VMEM((2 * tiles, span, LANES), bf16),
            pltpu.VMEM((2 * tiles, span, LANES), f32),
            pltpu.VMEM((2 * tiles, span - rows, LANES), bf16),
            pltpu.VMEM((2 * tiles, span - rows, LANES), bf16),
            pltpu.VMEM((tiles, RIM, LANES), bf16),
            pltpu.VMEM((tiles, RIM, LANES), bf16),
            pltpu.VMEM((tiles, rows, LANES), bf16),
            pltpu.VMEM((tiles, RIM, LANES), bf16),
            pltpu.VMEM((8, LANES), f32),
            pltpu.VMEM((REACH + 1, 8, LANES), f32),
            pltpu.VMEM((span, 2 * rows), f32),
            pltpu.VMEM((rows, LANES), f32),
            pltpu.VMEM((rows, LANES), f32),
            pltpu.VMEM((rows + RIM, LANES), f32),
            pltpu.VMEM((8, shifted_rows, LANES), f32),
            *[pltpu.VMEM((rows, width), bf16)] * 4,
            pltpu.VMEM((taps, width), f32),
            sems((5,)),
            pltpu.VMEM((tiles, span, 2 * rows), f32),
            pltpu.VMEM((taps, LANES), f32),
            pltpu.VMEM((n_dp, piece, LANES), bf16),
            pltpu.VMEM((n_dp, piece, LANES), bf16),
            pltpu.VMEM((piece, LANES), bf16),
            pltpu.VMEM((piece, LANES), bf16),
            pltpu.VMEM((QUAD, piece, LANES), bf16),
            pltpu.VMEM((rounds, piece, LANES), bf16),
            pltpu.VMEM((piece, LANES), bf16),
            pltpu.VMEM((n_dp, piece, LANES), bf16),
            sems((4,)), sems((4,)),
            sems((units, REACH)), sems((units, REACH)),
            sems((units, REACH)), sems((units, REACH)),
            sems((tiles // batch,)), sems((tiles // batch,)), sems((half,)), sems((half,)),
            sems((REACH + 1,)), sems((REACH + 1,)),
        ],
        compiler_params=pltpu.CompilerParams(
            collective_id=0, has_side_effects=True, vmem_limit_bytes=48 * 1024 * 1024
        ),
        name="timeline",
    )(query, key_rows, feats, grad, ids, picked, weight)


def per_device(queries, keys, events, out_grad, segment_ids, block_list, conv_weight):
    blist = block_list[0]
    here = lax.axis_index("seq")
    own = lax.dynamic_slice_in_dim(blist, here, 1, 0)
    wanted = here - jnp.arange(8, dtype=jnp.int32)
    hit = jnp.any(own == wanted[:, None], axis=1) & (wanted >= 0)
    picked = jnp.broadcast_to(hit.astype(jnp.float32)[:, None], (8, LANES))
    q_grad, k_grad, e_grad, f_grad = timeline(
        queries[0], keys[0], events[0], out_grad[0], segment_ids, picked, conv_weight
    )
    return (q_grad[None], k_grad[None], e_grad[None], f_grad)


def solution(mesh):
    in_specs = (
        P("dp", "seq", None),
        P("dp", "seq", None),
        P("dp", "seq", None),
        P("dp", "seq", None),
        P("dp", "seq"),
        P("dp", None, None),
        P(),
    )
    out_specs = (P("dp", "seq", None), P("dp", "seq", None), P("dp", "seq", None), P())
    return jax.shard_map(
        per_device, mesh=mesh, in_specs=in_specs, out_specs=out_specs, check_vma=False
    )
```

```python
import jax
import jax.numpy as jnp
from jax import lax
from jax.experimental import pallas as pl
from jax.experimental.pallas import tpu as pltpu
from jax.sharding import PartitionSpec as P

HD = 64
REACH = 4
LANES = 128
RIM = 64
BATCH = 4
PAIR = 2
QUAD = 4
MESH = pl.DeviceIdType.MESH


def timeline(query, key_rows, feats, grad, ids, blist, weight):
    n_dp, n_seq = lax.axis_size("dp"), lax.axis_size("seq")
    rows, width = query.shape
    taps = weight.shape[0]
    tiles = width // LANES
    batch = min(BATCH, tiles)
    half = tiles // PAIR
    units = 2 * half
    conv_lag = min(2, half - 1)
    rounds = n_seq // QUAD
    split = n_dp // tiles
    piece = taps // split
    mean = 1.0 / (n_dp * n_seq)
    scale = HD ** (-0.5)
    span = (REACH + 1) * rows
    shifted_rows = rows + RIM - 8
    f32, bf16 = jnp.float32, jnp.bfloat16

    def kernel(
        q_in, k_in, e_in, g_in, id_ref, list_ref, w_in,
        dq_ref, dk_ref, de_ref, f_out,
        win, part, out_buf, in_buf, e_halo, v_halo, vg, e_src,
        id_src, id_buf, cap, left, right, ext, moved,
        q_ref, k_ref, e_ref, g_ref, w_ref, load_s,
        probs_ref, f_ref, mine, got, near, far, near_in, far_in, total_sum, whole, sum_s, sum_r,
        win_s, win_r, back_s, back_r, eh_s, eh_r, vh_s, vh_r, id_s, id_r,
    ):
        me, lane_me = lax.axis_index("seq"), lax.axis_index("dp")

        def at(offset):
            return lax.rem(me + offset + n_seq, n_seq)

        up, down = at(1), at(-1)

        def remote(src, dst, send, recv, to):
            return pltpu.make_async_remote_copy(
                src_ref=src, dst_ref=dst, send_sem=send, recv_sem=recv,
                device_id={"seq": to}, device_id_type=MESH,
            )

        def cols(tile):
            return pl.ds(pl.multiple_of(tile * LANES, LANES), LANES)

        def both(u):
            return pl.ds(u * PAIR, PAIR)

        def fwd(u, d):
            return remote(
                win.at[both(u), pl.ds((d - 1) * rows, rows), :],
                win.at[both(u), pl.ds(d * rows, rows), :],
                win_s.at[u, d - 1], win_r.at[u, d - 1], up,
            )

        def back(u, d):
            return remote(
                out_buf.at[both(u), pl.ds((d - 1) * rows, rows), :],
                in_buf.at[both(u), pl.ds((d - 1) * rows, rows), :],
                back_s.at[u, d - 1], back_r.at[u, d - 1], down,
            )

        def events_halo(n):
            several = pl.ds(n * batch, batch)
            return remote(e_src.at[several], e_halo.at[several], eh_s.at[n], eh_r.at[n], up)

        def grads_halo(u):
            return remote(
                vg.at[both(u), pl.ds(0, RIM), :], v_halo.at[both(u)], vh_s.at[u], vh_r.at[u], down
            )

        def ids_to(slot):
            to = down if slot == 0 else at(slot)
            return remote(id_src, id_buf.at[slot], id_s.at[slot], id_r.at[slot], to)

        loads = [
            pltpu.make_async_copy(src, dst, load_s.at[n])
            for n, (src, dst) in enumerate(
                ((e_in, e_ref), (k_in, k_ref), (w_in, w_ref), (q_in, q_ref), (g_in, g_ref))
            )
        ]
        for load in loads:
            load.start()
        barrier = pltpu.get_barrier_semaphore()

        def greet_seq(n, _):
            pl.semaphore_signal(barrier, inc=1, device_id={"seq": at(n)}, device_id_type=MESH)
            return 0

        def greet_dp(n, _):
            to = lax.rem(lane_me + n, n_dp)
            pl.semaphore_signal(barrier, inc=1, device_id={"dp": to}, device_id_type=MESH)
            return 0

        lax.fori_loop(1, n_seq, greet_seq, 0)
        lax.fori_loop(1, n_dp, greet_dp, 0)
        own_ids = id_ref[...].astype(f32)
        id_src[...] = jnp.broadcast_to(own_ids, id_src.shape)

        for load in loads:
            load.wait()

        def stage(tile, _):
            win[tile, pl.ds(0, rows), :] = k_ref[:, cols(tile)]
            e_src[tile] = e_ref[pl.ds(rows - RIM, RIM), cols(tile)]
            return 0

        lax.fori_loop(0, tiles, stage, 0)
        pl.semaphore_wait(barrier, n_seq + n_dp - 2)
        for slot in range(REACH + 1):
            ids_to(slot).start()

        fwd(0, 1).start()
        for slot in range(REACH + 1):
            ids_to(slot).wait_recv()

        square = (rows, rows)
        own_row = jnp.broadcast_to(own_ids, square)

        def same(row):
            col = jnp.broadcast_to(row, square).T
            return jnp.where(col == own_row, 1.0, 0.0)

        s_at = lax.broadcasted_iota(jnp.int32, square, 0)
        r_at = lax.broadcasted_iota(jnp.int32, square, 1)
        here = same(own_ids)
        low = jnp.where(s_at <= r_at, here, 0.0)
        high = jnp.where(s_at >= r_at, here, 0.0)
        before = same(id_buf[1][0:1]) * jnp.where(me > 0, 1.0, 0.0)
        after = same(id_buf[0][0:1]) * jnp.where(me < n_seq - 1, 1.0, 0.0)
        reach_left = jnp.sum(low, axis=0, keepdims=True) + jnp.sum(before, axis=0, keepdims=True) - 1.0
        reach_right = jnp.sum(high, axis=0, keepdims=True) + jnp.sum(after, axis=0, keepdims=True) - 1.0
        left[...] = jnp.broadcast_to(reach_left, square).T
        right[...] = jnp.broadcast_to(reach_right, square).T
        listed = list_ref[pl.ds(me, 1), :]
        for d in range(REACH + 1):
            open_pairs = low if d == 0 else same(id_buf[d][0:1])
            wanted = jnp.where(listed == me - d, 1.0, 0.0)
            open_pairs = open_pairs * jnp.broadcast_to(
                jnp.max(wanted, axis=1, keepdims=True), square
            )
            limit = jnp.where(open_pairs > 0.5, 3.0e38, -1.0e30)
            cap[d * rows : (d + 1) * rows, 0:rows] = limit
            cap[d * rows : (d + 1) * rows, rows : 2 * rows] = limit

        def shift_back():
            for k in range(8):
                moved[k] = ext[8 - k : 8 - k + shifted_rows, :]

        def load_events(tile):
            ext[0:RIM, :] = e_halo[tile].astype(f32)
            ext[RIM : RIM + rows, :] = e_ref[:, cols(tile)].astype(f32)
            shift_back()

        def taps_at(q, tile):
            return w_ref[pl.ds(pl.multiple_of(q * 8, 8), 8), cols(tile)]

        def conv(tile):
            load_events(tile)
            reach = left[...]

            def body(q, total):
                tap_rows = taps_at(q, tile)
                base = pl.multiple_of(RIM - 8 - 8 * q, 8)
                first = (q * 8).astype(f32)
                for k in range(8):
                    piece = moved[k, pl.ds(base, rows), :]
                    total = total + jnp.where(reach >= first + k, piece * tap_rows[k : k + 1, :], 0.0)
                return total

            total = lax.fori_loop(0, taps // 8, body, jnp.zeros((rows, LANES), f32))
            win[tiles + tile, pl.ds(0, rows), :] = total.astype(bf16)

        def conv_next(tile):
            @pl.when(lax.rem(tile, batch) == 0)
            def _():
                events_halo(tile // batch).wait_recv()

            conv(tile)

        lane = lax.broadcasted_iota(jnp.int32, (rows, LANES), 1)
        first_head = lane < HD
        last = (((1,), (1,)), ((), ()))
        mid = (((1,), (0,)), ((), ()))

        def heads(ref, tile):
            wide = ref[:, cols(tile)].astype(f32)
            return jnp.concatenate(
                [jnp.where(first_head, wide, 0.0), jnp.where(first_head, 0.0, wide)], axis=0
            ).astype(bf16)

        def attend_keys(tile):
            scores = lax.dot_general(win[tile], heads(q_ref, tile), last, preferred_element_type=f32)
            scores = jnp.minimum(scores * scale, cap[...])
            top = jnp.max(scores, axis=0, keepdims=True)
            raw = jnp.exp(scores - top)
            probs = raw * (1.0 / jnp.sum(raw, axis=0, keepdims=True))
            probs_ref[tile] = probs
            part[tile] = lax.dot_general(
                probs.astype(bf16), heads(g_ref, tile), mid, preferred_element_type=f32
            )

        def attend_values(tile):
            keys, vals = win[tile], win[tiles + tile]
            probs = probs_ref[tile]
            dprobs = lax.dot_general(vals, heads(g_ref, tile), last, preferred_element_type=f32)
            low_probs = probs.astype(bf16).astype(f32)
            delta = jnp.sum(low_probs * dprobs, axis=0, keepdims=True)
            dscores = (probs * (dprobs - delta)).astype(bf16)
            part[tiles + tile] = scale * lax.dot_general(
                dscores, heads(q_ref, tile), mid, preferred_element_type=f32
            )
            dq2 = lax.dot_general(
                dscores, keys, (((0,), (0,)), ((), ())), preferred_element_type=f32
            )
            dq = jnp.where(first_head, dq2[0:rows], dq2[rows : 2 * rows]) * scale
            dq_ref[:, cols(tile)] = dq.astype(bf16)

        def give(u, d):
            at_d = pl.ds(d * rows, rows)
            total = part[both(u), at_d, :]
            if d < REACH:
                back(u, d + 1).wait_recv()
                total = total + in_buf[both(u), at_d, :].astype(f32)
            out_buf[both(u), pl.ds((d - 1) * rows, rows), :] = total.astype(bf16)
            back(u, d).start()

        def settle(u):
            back(u, 1).wait_recv()
            total = part[both(u), pl.ds(0, rows), :] + in_buf[both(u), pl.ds(0, rows), :].astype(f32)
            return total.astype(bf16)

        def settle_values(u):
            vg[both(u)] = settle(u)
            grads_halo(u).start()

        def settle_keys(u):
            low_total = settle(u)
            for n in range(PAIR):
                dk_ref[:, cols((u - half) * PAIR + n)] = low_total[n]

        def events_back(tile):
            own = vg[tile].astype(f32)
            ext[0:rows, :] = own
            ext[rows : rows + RIM, :] = v_halo[tile].astype(f32)
            for k in range(8):
                moved[k] = ext[k : k + shifted_rows, :]
            reach = right[...]

            def body(q, total):
                tap_rows = taps_at(q, tile)
                base = pl.multiple_of(8 * q, 8)
                first = (q * 8).astype(f32)
                for k in range(8):
                    piece = moved[k, pl.ds(base, rows), :]
                    total = total + jnp.where(reach >= first + k, piece * tap_rows[k : k + 1, :], 0.0)
                return total

            total = lax.fori_loop(0, taps // 8, body, jnp.zeros((rows, LANES), f32))
            de_ref[:, cols(tile)] = total.astype(bf16)

        def tap_sums(tile):
            own = vg[tile].astype(f32)
            load_events(tile)
            reach_l = left[...]

            def tap_body(q, _):
                base = pl.multiple_of(RIM - 8 - 8 * q, 8)
                first = (q * 8).astype(f32)
                sums = []
                for k in range(8):
                    piece = moved[k, pl.ds(base, rows), :]
                    kept = jnp.where(reach_l >= first + k, piece * own, 0.0)
                    sums.append(jnp.sum(kept, axis=0, keepdims=True))
                f_ref[pl.ds(pl.multiple_of(q * 8, 8), 8), :] = jnp.concatenate(sums, axis=0)
                return 0

            lax.fori_loop(0, taps // 8, tap_body, 0)
            share(tile)

        def to_dp(src, dst, n, to):
            return pltpu.make_async_remote_copy(
                src_ref=src, dst_ref=dst, send_sem=sum_s.at[n], recv_sem=sum_r.at[n],
                device_id={"dp": to}, device_id_type=MESH,
            )

        def share(tile):
            for h in range(split):
                owner = tile * split + h
                mine[owner] = f_ref[h * piece : (h + 1) * piece, :].astype(bf16)

                @pl.when(owner == lane_me)
                def _():
                    got[owner] = mine[owner]

                @pl.when(owner != lane_me)
                def _():
                    to_dp(mine.at[owner], got.at[lane_me], 0, owner).start()

        def settled(ref, n, count):
            pltpu.make_async_copy(ref.at[pl.ds(0, count)], ref.at[pl.ds(0, count)], n).wait()

        my_quad, my_place = lax.div(me, QUAD), lax.rem(me, QUAD)

        def added(ref, count):
            total = ref[0].astype(f32)
            for n in range(1, count):
                total = total + ref[n].astype(f32)
            return total

        def sum_near():
            settled(got, sum_r.at[0], n_dp - 1)
            near[...] = added(got, n_dp).astype(bf16)
            near_in[my_place] = near[...]
            for n in range(1, QUAD):
                to = my_quad * QUAD + lax.rem(my_place + n, QUAD)
                remote(near, near_in.at[my_place], sum_s.at[1], sum_r.at[1], to).start()

        def sum_far():
            settled(near_in, sum_r.at[1], QUAD - 1)
            far[...] = added(near_in, QUAD).astype(bf16)
            far_in[my_quad] = far[...]
            for n in range(1, rounds):
                remote(far, far_in.at[my_quad], sum_s.at[2], sum_r.at[2], at(n * QUAD)).start()

        def send_dp(n, _):
            to_dp(total_sum, whole.at[lane_me], 3, lax.rem(lane_me + n, n_dp)).start()
            return 0

        def sum_out():
            settled(far_in, sum_r.at[2], rounds - 1)
            total_sum[...] = (added(far_in, rounds) * mean).astype(bf16)
            whole[lane_me] = total_sum[...]
            lax.fori_loop(1, n_dp // 2, send_dp, 0)

        def sum_end():
            settled(whole, sum_r.at[3], n_dp - 1)
            for n in range(n_dp):
                col, row = (n // split) * LANES, (n % split) * piece
                f_out[row : row + piece, col : col + LANES] = whole[n].astype(f32)
            settled(mine, sum_s.at[0], n_dp - 1)
            settled(near_in, sum_s.at[1], QUAD - 1)
            settled(far_in, sum_s.at[2], rounds - 1)
            settled(whole, sum_s.at[3], n_dp - 1)

        def each(act, first):
            def body(n, _):
                act(first + n)
                return 0

            lax.fori_loop(0, PAIR, body, 0)

        def meet_keys(u):
            fwd(u, REACH).wait_recv()
            for n in range(PAIR):
                attend_keys(u * PAIR + n)

        def meet_values(u):
            fwd(u, REACH).wait_recv()
            for n in range(PAIR):
                attend_values((u - half) * PAIR + n)

        def values_done(u):
            settle_values(u)
            each(tap_sums, u * PAIR)

        def events_pair(u):
            grads_halo(u).wait_recv()
            each(events_back, u * PAIR)

        def pass_on(u, d):
            fwd(u, d - 1).wait_recv()
            fwd(u, d).start()

        summed = half + 8

        def tick(i, _):
            def on(u, act, low_end=0, high_end=units):
                @pl.when(jnp.logical_and(u >= low_end, u < high_end))
                def _():
                    act(u)

            on(i, lambda u: fwd(u, 1).start(), low_end=1)
            on(i, lambda n: events_halo(n).start(), high_end=tiles // batch)
            on(i - 1, lambda u: pass_on(u, 2))
            on(i - 5, lambda u: give(u, 4))
            on(i - 2, lambda u: pass_on(u, 3))
            on(i - 6, lambda u: give(u, 3))
            on(i - 3, lambda u: pass_on(u, 4))
            on(i - 7, lambda u: give(u, 2))
            on(i - 8, lambda u: give(u, 1))
            on(i - conv_lag, lambda p: each(conv_next, p * PAIR), high_end=half)
            on(i - 9, values_done, high_end=half)
            on(i - 9, settle_keys, low_end=half)
            on(i - 11, events_pair, high_end=half)
            pl.when(i == summed + 2)(sum_near)
            pl.when(i == summed + 3)(sum_far)
            pl.when(i == summed + 5)(sum_out)

            @pl.when(i == summed + 6)
            def _():
                lax.fori_loop(n_dp // 2, n_dp, send_dp, 0)

            on(i - 4, meet_keys, high_end=half)
            on(i - 4, meet_values, low_end=half)
            return 0

        lax.fori_loop(0, max(units + 9, summed + 7), tick, 0)
        sum_end()
        for slot in range(REACH + 1):
            ids_to(slot).wait_send()

        def drain(u, _):
            for d in range(1, REACH + 1):
                fwd(u, d).wait_send()
                back(u, d).wait_send()
            return 0

        def drain_grads(u, _):
            grads_halo(u).wait_send()
            return 0

        def drain_halo(n, _):
            events_halo(n).wait_send()
            return 0

        lax.fori_loop(0, units, drain, 0)
        lax.fori_loop(0, half, drain_grads, 0)
        lax.fori_loop(0, tiles // batch, drain_halo, 0)

    vmem = pl.BlockSpec(memory_space=pltpu.VMEM)
    hbm = pl.BlockSpec(memory_space=pltpu.HBM)
    sems = pltpu.SemaphoreType.DMA
    tall = jax.ShapeDtypeStruct((rows, width), bf16)
    return pl.pallas_call(
        kernel,
        out_shape=(tall, tall, tall, jax.ShapeDtypeStruct((taps, width), f32)),
        in_specs=[hbm] * 4 + [vmem, vmem, hbm],
        out_specs=(vmem,) * 4,
        scratch_shapes=[
            pltpu.VMEM((2 * tiles, span, LANES), bf16),
            pltpu.VMEM((2 * tiles, span, LANES), f32),
            pltpu.VMEM((2 * tiles, span - rows, LANES), bf16),
            pltpu.VMEM((2 * tiles, span - rows, LANES), bf16),
            pltpu.VMEM((tiles, RIM, LANES), bf16),
            pltpu.VMEM((tiles, RIM, LANES), bf16),
            pltpu.VMEM((tiles, rows, LANES), bf16),
            pltpu.VMEM((tiles, RIM, LANES), bf16),
            pltpu.VMEM((8, LANES), f32),
            pltpu.VMEM((REACH + 1, 8, LANES), f32),
            pltpu.VMEM((span, 2 * rows), f32),
            pltpu.VMEM((rows, LANES), f32),
            pltpu.VMEM((rows, LANES), f32),
            pltpu.VMEM((rows + RIM, LANES), f32),
            pltpu.VMEM((8, shifted_rows, LANES), f32),
            *[pltpu.VMEM((rows, width), bf16)] * 4,
            pltpu.VMEM((taps, width), f32),
            sems((5,)),
            pltpu.VMEM((tiles, span, 2 * rows), f32),
            pltpu.VMEM((taps, LANES), f32),
            pltpu.VMEM((n_dp, piece, LANES), bf16),
            pltpu.VMEM((n_dp, piece, LANES), bf16),
            pltpu.VMEM((piece, LANES), bf16),
            pltpu.VMEM((piece, LANES), bf16),
            pltpu.VMEM((QUAD, piece, LANES), bf16),
            pltpu.VMEM((rounds, piece, LANES), bf16),
            pltpu.VMEM((piece, LANES), bf16),
            pltpu.VMEM((n_dp, piece, LANES), bf16),
            sems((4,)), sems((4,)),
            sems((units, REACH)), sems((units, REACH)),
            sems((units, REACH)), sems((units, REACH)),
            sems((tiles // batch,)), sems((tiles // batch,)), sems((half,)), sems((half,)),
            sems((REACH + 1,)), sems((REACH + 1,)),
        ],
        compiler_params=pltpu.CompilerParams(
            collective_id=0, has_side_effects=True, vmem_limit_bytes=63 * 1024 * 1024
        ),
        name="timeline",
    )(query, key_rows, feats, grad, ids, blist, weight)


def per_device(queries, keys, events, out_grad, segment_ids, block_list, conv_weight):
    q_grad, k_grad, e_grad, f_grad = timeline(
        queries[0], keys[0], events[0], out_grad[0], segment_ids, block_list[0], conv_weight
    )
    return (q_grad[None], k_grad[None], e_grad[None], f_grad)


def solution(mesh):
    in_specs = (
        P("dp", "seq", None),
        P("dp", "seq", None),
        P("dp", "seq", None),
        P("dp", "seq", None),
        P("dp", "seq"),
        P("dp", None, None),
        P(),
    )
    out_specs = (P("dp", "seq", None), P("dp", "seq", None), P("dp", "seq", None), P())
    return jax.shard_map(
        per_device, mesh=mesh, in_specs=in_specs, out_specs=out_specs, check_vma=False
    )
```

```python
import jax
import jax.numpy as jnp
from jax import lax
from jax.experimental import pallas as pl
from jax.experimental.pallas import tpu as pltpu
from jax.sharding import PartitionSpec as P

HD = 64
REACH = 4
LANES = 128
RIM = 64
BATCH = 4
PAIR = 2
QUAD = 4
MESH = pl.DeviceIdType.MESH


def timeline(query, key_rows, feats, grad, ids, blist, weight):
    n_dp, n_seq = lax.axis_size("dp"), lax.axis_size("seq")
    rows, width = query.shape
    taps = weight.shape[0]
    tiles = width // LANES
    batch = min(BATCH, tiles)
    half = tiles // PAIR
    units = 2 * half
    conv_lag = min(2, half - 1)
    rounds = n_seq // QUAD
    split = n_dp // tiles
    piece = taps // split
    mean = 1.0 / (n_dp * n_seq)
    scale = HD ** (-0.5)
    span = (REACH + 1) * rows
    shifted_rows = rows + RIM - 8
    f32, bf16 = jnp.float32, jnp.bfloat16

    def kernel(
        q_in, k_in, e_in, g_in, id_ref, list_ref, w_in,
        dq_ref, dk_ref, de_ref, f_out,
        win, part, out_buf, in_buf, e_halo, v_halo, vg, e_src,
        id_src, id_buf, cap, left, right, ext, moved,
        q_ref, k_ref, e_ref, g_ref, w_ref, load_s,
        probs_ref, f_ref, mine, got, near, far, near_in, far_in, total_sum, whole, sum_s, sum_r,
        win_s, win_r, back_s, back_r, eh_s, eh_r, vh_s, vh_r, id_s, id_r,
    ):
        me, lane_me = lax.axis_index("seq"), lax.axis_index("dp")

        def at(offset):
            return lax.rem(me + offset + n_seq, n_seq)

        up, down = at(1), at(-1)

        def remote(src, dst, send, recv, to):
            return pltpu.make_async_remote_copy(
                src_ref=src, dst_ref=dst, send_sem=send, recv_sem=recv,
                device_id={"seq": to}, device_id_type=MESH,
            )

        def cols(tile):
            return pl.ds(pl.multiple_of(tile * LANES, LANES), LANES)

        def both(u):
            return pl.ds(u * PAIR, PAIR)

        def fwd(u, d):
            return remote(
                win.at[both(u), pl.ds((d - 1) * rows, rows), :],
                win.at[both(u), pl.ds(d * rows, rows), :],
                win_s.at[u, d - 1], win_r.at[u, d - 1], up,
            )

        def back(u, d):
            return remote(
                out_buf.at[both(u), pl.ds((d - 1) * rows, rows), :],
                in_buf.at[both(u), pl.ds((d - 1) * rows, rows), :],
                back_s.at[u, d - 1], back_r.at[u, d - 1], down,
            )

        def events_halo(n):
            several = pl.ds(n * batch, batch)
            return remote(e_src.at[several], e_halo.at[several], eh_s.at[n], eh_r.at[n], up)

        def grads_halo(u):
            return remote(
                vg.at[both(u), pl.ds(0, RIM), :], v_halo.at[both(u)], vh_s.at[u], vh_r.at[u], down
            )

        def ids_to(slot):
            to = down if slot == 0 else at(slot)
            return remote(id_src, id_buf.at[slot], id_s.at[slot], id_r.at[slot], to)

        loads = [
            pltpu.make_async_copy(src, dst, load_s.at[n])
            for n, (src, dst) in enumerate(
                ((e_in, e_ref), (k_in, k_ref), (w_in, w_ref), (q_in, q_ref), (g_in, g_ref))
            )
        ]
        for load in loads:
            load.start()
        barrier = pltpu.get_barrier_semaphore()

        def greet_seq(n, _):
            pl.semaphore_signal(barrier, inc=1, device_id={"seq": at(n)}, device_id_type=MESH)
            return 0

        def greet_dp(n, _):
            to = lax.rem(lane_me + n, n_dp)
            pl.semaphore_signal(barrier, inc=1, device_id={"dp": to}, device_id_type=MESH)
            return 0

        lax.fori_loop(1, n_seq, greet_seq, 0)
        lax.fori_loop(1, n_dp, greet_dp, 0)
        own_ids = id_ref[...].astype(f32)
        id_src[...] = jnp.broadcast_to(own_ids, id_src.shape)

        for load in loads:
            load.wait()

        def stage(tile, _):
            win[tile, pl.ds(0, rows), :] = k_ref[:, cols(tile)]
            e_src[tile] = e_ref[pl.ds(rows - RIM, RIM), cols(tile)]
            return 0

        lax.fori_loop(0, tiles, stage, 0)
        pl.semaphore_wait(barrier, n_seq + n_dp - 2)
        for slot in range(REACH + 1):
            ids_to(slot).start()

        fwd(0, 1).start()
        for slot in range(REACH + 1):
            ids_to(slot).wait_recv()

        square = (rows, rows)
        own_row = jnp.broadcast_to(own_ids, square)

        def same(row):
            col = jnp.broadcast_to(row, square).T
            return jnp.where(col == own_row, 1.0, 0.0)

        s_at = lax.broadcasted_iota(jnp.int32, square, 0)
        r_at = lax.broadcasted_iota(jnp.int32, square, 1)
        here = same(own_ids)
        low = jnp.where(s_at <= r_at, here, 0.0)
        high = jnp.where(s_at >= r_at, here, 0.0)
        before = same(id_buf[1][0:1]) * jnp.where(me > 0, 1.0, 0.0)
        after = same(id_buf[0][0:1]) * jnp.where(me < n_seq - 1, 1.0, 0.0)
        reach_left = jnp.sum(low, axis=0, keepdims=True) + jnp.sum(before, axis=0, keepdims=True) - 1.0
        reach_right = jnp.sum(high, axis=0, keepdims=True) + jnp.sum(after, axis=0, keepdims=True) - 1.0
        left[...] = jnp.broadcast_to(reach_left, square).T
        right[...] = jnp.broadcast_to(reach_right, square).T
        listed = list_ref[...]
        mine_at = lax.broadcasted_iota(jnp.int32, listed.shape, 1) == me
        for d in range(REACH + 1):
            open_pairs = low if d == 0 else same(id_buf[d][0:1])
            wanted = jnp.where(mine_at & (listed == me - d), 1.0, 0.0)
            wanted = jnp.max(wanted, axis=0, keepdims=True)
            open_pairs = open_pairs * jnp.broadcast_to(
                jnp.max(wanted, axis=1, keepdims=True), square
            )
            limit = jnp.where(open_pairs > 0.5, 3.0e38, -1.0e30)
            cap[d * rows : (d + 1) * rows, 0:rows] = limit
            cap[d * rows : (d + 1) * rows, rows : 2 * rows] = limit

        def shift_back():
            for k in range(8):
                moved[k] = ext[8 - k : 8 - k + shifted_rows, :]

        def load_events(tile):
            ext[0:RIM, :] = e_halo[tile].astype(f32)
            ext[RIM : RIM + rows, :] = e_ref[:, cols(tile)].astype(f32)
            shift_back()

        def taps_at(q, tile):
            return w_ref[pl.ds(pl.multiple_of(q * 8, 8), 8), cols(tile)]

        def conv(tile):
            load_events(tile)
            reach = left[...]

            def body(q, total):
                tap_rows = taps_at(q, tile)
                base = pl.multiple_of(RIM - 8 - 8 * q, 8)
                first = (q * 8).astype(f32)
                for k in range(8):
                    piece = moved[k, pl.ds(base, rows), :]
                    total = total + jnp.where(reach >= first + k, piece * tap_rows[k : k + 1, :], 0.0)
                return total

            total = lax.fori_loop(0, taps // 8, body, jnp.zeros((rows, LANES), f32))
            win[tiles + tile, pl.ds(0, rows), :] = total.astype(bf16)

        def conv_next(tile):
            @pl.when(lax.rem(tile, batch) == 0)
            def _():
                events_halo(tile // batch).wait_recv()

            conv(tile)

        lane = lax.broadcasted_iota(jnp.int32, (rows, LANES), 1)
        first_head = lane < HD
        last = (((1,), (1,)), ((), ()))
        mid = (((1,), (0,)), ((), ()))

        def heads(ref, tile):
            wide = ref[:, cols(tile)].astype(f32)
            return jnp.concatenate(
                [jnp.where(first_head, wide, 0.0), jnp.where(first_head, 0.0, wide)], axis=0
            ).astype(bf16)

        def attend_keys(tile):
            scores = lax.dot_general(win[tile], heads(q_ref, tile), last, preferred_element_type=f32)
            scores = jnp.minimum(scores * scale, cap[...])
            top = jnp.max(scores, axis=0, keepdims=True)
            raw = jnp.exp(scores - top)
            probs = raw * (1.0 / jnp.sum(raw, axis=0, keepdims=True))
            probs_ref[tile] = probs
            part[tile] = lax.dot_general(
                probs.astype(bf16), heads(g_ref, tile), mid, preferred_element_type=f32
            )

        def attend_values(tile):
            keys, vals = win[tile], win[tiles + tile]
            probs = probs_ref[tile]
            dprobs = lax.dot_general(vals, heads(g_ref, tile), last, preferred_element_type=f32)
            low_probs = probs.astype(bf16).astype(f32)
            delta = jnp.sum(low_probs * dprobs, axis=0, keepdims=True)
            dscores = (probs * (dprobs - delta)).astype(bf16)
            part[tiles + tile] = scale * lax.dot_general(
                dscores, heads(q_ref, tile), mid, preferred_element_type=f32
            )
            dq2 = lax.dot_general(
                dscores, keys, (((0,), (0,)), ((), ())), preferred_element_type=f32
            )
            dq = jnp.where(first_head, dq2[0:rows], dq2[rows : 2 * rows]) * scale
            dq_ref[:, cols(tile)] = dq.astype(bf16)

        def give(u, d):
            at_d = pl.ds(d * rows, rows)
            total = part[both(u), at_d, :]
            if d < REACH:
                back(u, d + 1).wait_recv()
                total = total + in_buf[both(u), at_d, :].astype(f32)
            out_buf[both(u), pl.ds((d - 1) * rows, rows), :] = total.astype(bf16)
            back(u, d).start()

        def settle(u):
            back(u, 1).wait_recv()
            total = part[both(u), pl.ds(0, rows), :] + in_buf[both(u), pl.ds(0, rows), :].astype(f32)
            return total.astype(bf16)

        def settle_values(u):
            vg[both(u)] = settle(u)
            grads_halo(u).start()

        def settle_keys(u):
            low_total = settle(u)
            for n in range(PAIR):
                dk_ref[:, cols((u - half) * PAIR + n)] = low_total[n]

        def events_back(tile):
            own = vg[tile].astype(f32)
            ext[0:rows, :] = own
            ext[rows : rows + RIM, :] = v_halo[tile].astype(f32)
            for k in range(8):
                moved[k] = ext[k : k + shifted_rows, :]
            reach = right[...]

            def body(q, total):
                tap_rows = taps_at(q, tile)
                base = pl.multiple_of(8 * q, 8)
                first = (q * 8).astype(f32)
                for k in range(8):
                    piece = moved[k, pl.ds(base, rows), :]
                    total = total + jnp.where(reach >= first + k, piece * tap_rows[k : k + 1, :], 0.0)
                return total

            total = lax.fori_loop(0, taps // 8, body, jnp.zeros((rows, LANES), f32))
            de_ref[:, cols(tile)] = total.astype(bf16)

        def tap_sums(tile):
            own = vg[tile].astype(f32)
            load_events(tile)
            reach_l = left[...]

            def tap_body(q, _):
                base = pl.multiple_of(RIM - 8 - 8 * q, 8)
                first = (q * 8).astype(f32)
                sums = []
                for k in range(8):
                    piece = moved[k, pl.ds(base, rows), :]
                    kept = jnp.where(reach_l >= first + k, piece * own, 0.0)
                    sums.append(jnp.sum(kept, axis=0, keepdims=True))
                f_ref[pl.ds(pl.multiple_of(q * 8, 8), 8), :] = jnp.concatenate(sums, axis=0)
                return 0

            lax.fori_loop(0, taps // 8, tap_body, 0)
            share(tile)

        def to_dp(src, dst, n, to):
            return pltpu.make_async_remote_copy(
                src_ref=src, dst_ref=dst, send_sem=sum_s.at[n], recv_sem=sum_r.at[n],
                device_id={"dp": to}, device_id_type=MESH,
            )

        def share(tile):
            for h in range(split):
                owner = tile * split + h
                mine[owner] = f_ref[h * piece : (h + 1) * piece, :].astype(bf16)

                @pl.when(owner == lane_me)
                def _():
                    got[owner] = mine[owner]

                @pl.when(owner != lane_me)
                def _():
                    to_dp(mine.at[owner], got.at[lane_me], 0, owner).start()

        def settled(ref, n, count):
            pltpu.make_async_copy(ref.at[pl.ds(0, count)], ref.at[pl.ds(0, count)], n).wait()

        my_quad, my_place = lax.div(me, QUAD), lax.rem(me, QUAD)

        def added(ref, count):
            total = ref[0].astype(f32)
            for n in range(1, count):
                total = total + ref[n].astype(f32)
            return total

        def sum_near():
            settled(got, sum_r.at[0], n_dp - 1)
            near[...] = added(got, n_dp).astype(bf16)
            near_in[my_place] = near[...]
            for n in range(1, QUAD):
                to = my_quad * QUAD + lax.rem(my_place + n, QUAD)
                remote(near, near_in.at[my_place], sum_s.at[1], sum_r.at[1], to).start()

        def sum_far():
            settled(near_in, sum_r.at[1], QUAD - 1)
            far[...] = added(near_in, QUAD).astype(bf16)
            far_in[my_quad] = far[...]
            for n in range(1, rounds):
                remote(far, far_in.at[my_quad], sum_s.at[2], sum_r.at[2], at(n * QUAD)).start()

        def send_dp(n, _):
            to_dp(total_sum, whole.at[lane_me], 3, lax.rem(lane_me + n, n_dp)).start()
            return 0

        def sum_out():
            settled(far_in, sum_r.at[2], rounds - 1)
            total_sum[...] = (added(far_in, rounds) * mean).astype(bf16)
            whole[lane_me] = total_sum[...]
            lax.fori_loop(1, n_dp // 2, send_dp, 0)

        def sum_end():
            settled(whole, sum_r.at[3], n_dp - 1)
            for n in range(n_dp):
                col, row = (n // split) * LANES, (n % split) * piece
                f_out[row : row + piece, col : col + LANES] = whole[n].astype(f32)
            settled(mine, sum_s.at[0], n_dp - 1)
            settled(near_in, sum_s.at[1], QUAD - 1)
            settled(far_in, sum_s.at[2], rounds - 1)
            settled(whole, sum_s.at[3], n_dp - 1)

        def each(act, first):
            def body(n, _):
                act(first + n)
                return 0

            lax.fori_loop(0, PAIR, body, 0)

        def meet_keys(u):
            fwd(u, REACH).wait_recv()
            for n in range(PAIR):
                attend_keys(u * PAIR + n)

        def meet_values(u):
            fwd(u, REACH).wait_recv()
            for n in range(PAIR):
                attend_values((u - half) * PAIR + n)

        def values_done(u):
            settle_values(u)
            each(tap_sums, u * PAIR)

        def events_pair(u):
            grads_halo(u).wait_recv()
            each(events_back, u * PAIR)

        def pass_on(u, d):
            fwd(u, d - 1).wait_recv()
            fwd(u, d).start()

        summed = half + 8

        def tick(i, _):
            def on(u, act, low_end=0, high_end=units):
                @pl.when(jnp.logical_and(u >= low_end, u < high_end))
                def _():
                    act(u)

            on(i, lambda u: fwd(u, 1).start(), low_end=1)
            on(i, lambda n: events_halo(n).start(), high_end=tiles // batch)
            on(i - 1, lambda u: pass_on(u, 2))
            on(i - 5, lambda u: give(u, 4))
            on(i - 2, lambda u: pass_on(u, 3))
            on(i - 6, lambda u: give(u, 3))
            on(i - 3, lambda u: pass_on(u, 4))
            on(i - 7, lambda u: give(u, 2))
            on(i - 8, lambda u: give(u, 1))
            on(i - conv_lag, lambda p: each(conv_next, p * PAIR), high_end=half)
            on(i - 9, values_done, high_end=half)
            on(i - 9, settle_keys, low_end=half)
            on(i - 11, events_pair, high_end=half)
            pl.when(i == summed + 2)(sum_near)
            pl.when(i == summed + 3)(sum_far)
            pl.when(i == summed + 5)(sum_out)

            @pl.when(i == summed + 6)
            def _():
                lax.fori_loop(n_dp // 2, n_dp, send_dp, 0)

            on(i - 4, meet_keys, high_end=half)
            on(i - 4, meet_values, low_end=half)
            return 0

        lax.fori_loop(0, max(units + 9, summed + 7), tick, 0)
        sum_end()
        for slot in range(REACH + 1):
            ids_to(slot).wait_send()

        def drain(u, _):
            for d in range(1, REACH + 1):
                fwd(u, d).wait_send()
                back(u, d).wait_send()
            return 0

        def drain_grads(u, _):
            grads_halo(u).wait_send()
            return 0

        def drain_halo(n, _):
            events_halo(n).wait_send()
            return 0

        lax.fori_loop(0, units, drain, 0)
        lax.fori_loop(0, half, drain_grads, 0)
        lax.fori_loop(0, tiles // batch, drain_halo, 0)

    vmem = pl.BlockSpec(memory_space=pltpu.VMEM)
    hbm = pl.BlockSpec(memory_space=pltpu.HBM)
    sems = pltpu.SemaphoreType.DMA
    tall = jax.ShapeDtypeStruct((rows, width), bf16)
    return pl.pallas_call(
        kernel,
        out_shape=(tall, tall, tall, jax.ShapeDtypeStruct((taps, width), f32)),
        in_specs=[hbm] * 4 + [vmem, vmem, hbm],
        out_specs=(vmem,) * 4,
        scratch_shapes=[
            pltpu.VMEM((2 * tiles, span, LANES), bf16),
            pltpu.VMEM((2 * tiles, span, LANES), f32),
            pltpu.VMEM((2 * tiles, span - rows, LANES), bf16),
            pltpu.VMEM((2 * tiles, span - rows, LANES), bf16),
            pltpu.VMEM((tiles, RIM, LANES), bf16),
            pltpu.VMEM((tiles, RIM, LANES), bf16),
            pltpu.VMEM((tiles, rows, LANES), bf16),
            pltpu.VMEM((tiles, RIM, LANES), bf16),
            pltpu.VMEM((8, LANES), f32),
            pltpu.VMEM((REACH + 1, 8, LANES), f32),
            pltpu.VMEM((span, 2 * rows), f32),
            pltpu.VMEM((rows, LANES), f32),
            pltpu.VMEM((rows, LANES), f32),
            pltpu.VMEM((rows + RIM, LANES), f32),
            pltpu.VMEM((8, shifted_rows, LANES), f32),
            *[pltpu.VMEM((rows, width), bf16)] * 4,
            pltpu.VMEM((taps, width), f32),
            sems((5,)),
            pltpu.VMEM((tiles, span, 2 * rows), f32),
            pltpu.VMEM((taps, LANES), f32),
            pltpu.VMEM((n_dp, piece, LANES), bf16),
            pltpu.VMEM((n_dp, piece, LANES), bf16),
            pltpu.VMEM((piece, LANES), bf16),
            pltpu.VMEM((piece, LANES), bf16),
            pltpu.VMEM((QUAD, piece, LANES), bf16),
            pltpu.VMEM((rounds, piece, LANES), bf16),
            pltpu.VMEM((piece, LANES), bf16),
            pltpu.VMEM((n_dp, piece, LANES), bf16),
            sems((4,)), sems((4,)),
            sems((units, REACH)), sems((units, REACH)),
            sems((units, REACH)), sems((units, REACH)),
            sems((tiles // batch,)), sems((tiles // batch,)), sems((half,)), sems((half,)),
            sems((REACH + 1,)), sems((REACH + 1,)),
        ],
        compiler_params=pltpu.CompilerParams(
            collective_id=0, has_side_effects=True, vmem_limit_bytes=52 * 1024 * 1024
        ),
        name="timeline",
    )(query, key_rows, feats, grad, ids, blist, weight)


def per_device(queries, keys, events, out_grad, segment_ids, block_list, conv_weight):
    q_grad, k_grad, e_grad, f_grad = timeline(
        queries[0], keys[0], events[0], out_grad[0], segment_ids, block_list[0].T, conv_weight
    )
    return (q_grad[None], k_grad[None], e_grad[None], f_grad)


def solution(mesh):
    in_specs = (
        P("dp", "seq", None),
        P("dp", "seq", None),
        P("dp", "seq", None),
        P("dp", "seq", None),
        P("dp", "seq"),
        P("dp", None, None),
        P(),
    )
    out_specs = (P("dp", "seq", None), P("dp", "seq", None), P("dp", "seq", None), P())
    return jax.shard_map(
        per_device, mesh=mesh, in_specs=in_specs, out_specs=out_specs, check_vma=False
    )
```
